256 devices in a mesh: rows: 16 (over y, x), cols: 16 (over z, core).
Axes of the slice: x: 4, y: 4, z: 8, core: 2. Of those that a mesh axis runs over, the one named last changes fastest.
Arguments:
- design: float32 [6, 32, 128], P(None, 'rows', 'cols'), may hold values from -6 to 6
- active: int32 [32, 128], P('rows', 'cols'), may hold values 0 or 1
- stamp_basis: float32 [6, 32, 32], replicated, may hold values from -2 to 2
- film_field: bfloat16 [16, 512, 2048], P(None, 'rows', 'cols'), may hold values from -6 to 6
- lift_weight: float32 [16], replicated, may hold values from -4 to 4
- lift_bias: float32 [16], replicated, may hold values from -3 to 3
- conv_weight: bfloat16 [4, 9, 16, 16], replicated, may hold values from -0.5 to 0.5
- conv_bias: float32 [4, 16], replicated, may hold values from -3 to 3
- readout: float32 [16], replicated, may hold values from -1.5 to 1.5
- target: float32 [512, 2048], P('rows', 'cols'), may hold values from -6 to 6
- dilation: int32 [4], replicated, may hold values from 1 to 8, as said below
Outputs:
- new_design: float32 [6, 32, 128], P(None, 'rows', 'cols')
- objective: float32 [2], replicated
The draws below stay inside these ranges and needn't reach their ends.
Inputs may be any that keep to these rules, and one draw needn't show every extreme that they name: The dilation of each layer is an integer from 1 to 8; some layer has exactly 8.
All inputs are finite; a program needn't handle non-finite values. No bound on the sum of `active` on one device may be relied on, other than what follows from the above.
Results may differ from the reference program's by a relative error of at most 0.0025.
Values may be sent and summed in bfloat16 or wider, within the bound.
No kernel may reach another device: no remote copies, remote signals or barrier semaphores. Data moves between devices by JAX's collectives and lax.ppermute only.
A program may use at most 64 MiB of HBM per device.

```python
import jax
import jax.numpy as jnp
from jax import lax

CHANNELS = 16
NPARAM = 6
STRIDE = 16
DMAX = 8
LAYERS = 4
ITERS = 2
GR = 32
GC = 128
NR = 512
NC = 2048


def draw_dilation(key, part):
    levels = jax.random.randint(key, (LAYERS,), 1, DMAX + 1)
    chosen = jax.random.randint(jax.random.fold_in(key, 11), (), 0, LAYERS)
    return jnp.where(jnp.arange(LAYERS) == chosen, DMAX, levels).astype(jnp.int32)


def set_ends(array, own_key, low, largest):
    longest = array.shape.index(max(array.shape))
    spots = []
    for shift in (0, 1):
        where = [jax.random.randint(jax.random.fold_in(own_key, axis), (), 0, length) for axis, length in enumerate(array.shape)]
        where[longest] = (where[longest] + shift) % array.shape[longest]
        spots.append(tuple(where))
    return array.at[spots[0]].set(low).at[spots[1]].set(largest)


def shard_levels(key, shape, split, least, largest):
    level = 1.0
    for dim, parts in split:
        heights = jax.random.uniform(jax.random.fold_in(jax.random.fold_in(key, 6), dim), (parts,), jnp.float32, least / len(split), largest / len(split))
        level = level * jnp.repeat(jnp.exp(heights), shape[dim] // parts).reshape((-1,) + (1,) * (len(shape) - 1 - dim))
    return level


def normal_values(own_key, shape, deviation, limit, cuts=(), kind=jnp.bfloat16):
    values = deviation * jax.random.normal(own_key, shape, jnp.float32)
    if cuts:
        values = values * shard_levels(own_key, shape, cuts, -0.22, 0.18)
    return jnp.clip(values, -limit, limit).astype(kind)


def setup_inputs(seed: int = 0) -> dict:
    key_list = jax.random.split(jax.random.key(seed), 12)
    return {
        "design": normal_values(key_list[0], (NPARAM, GR, GC), 1.0, 6.0, ((1, 16), (2, 16)), jnp.float32),
        "active": set_ends((jax.random.randint(key_list[1], (GR, GC), 0, 4) < 3).astype(jnp.int32), jax.random.fold_in(key_list[1], 1), 0, 1),
        "stamp_basis": normal_values(key_list[2], (NPARAM, 2 * STRIDE, 2 * STRIDE), 0.25, 2.0, (), jnp.float32),
        "film_field": normal_values(key_list[3], (CHANNELS, NR, NC), 1.0, 6.0, ((1, 16), (2, 16))),
        "lift_weight": normal_values(key_list[4], (CHANNELS,), 1.0, 4.0, (), jnp.float32),
        "lift_bias": normal_values(key_list[5], (CHANNELS,), 0.5, 3.0, (), jnp.float32),
        "conv_weight": normal_values(key_list[6], (LAYERS, 9, CHANNELS, CHANNELS), (9 * CHANNELS) ** -0.5, 0.5),
        "conv_bias": normal_values(key_list[7], (LAYERS, CHANNELS), 0.5, 3.0, (), jnp.float32),
        "readout": normal_values(key_list[8], (CHANNELS,), CHANNELS ** -0.5, 1.5, (), jnp.float32),
        "target": normal_values(key_list[9], (NR, NC), 1.0, 6.0, ((0, 16), (1, 16)), jnp.float32),
        "dilation": draw_dilation(jax.random.fold_in(key_list[11], 71), 0),
    }


step_rate = 0.25
norm_eps = 1e-06

def tap_list():
    return [(row_step, col_step) for row_step in (-1, 0, 1) for col_step in (-1, 0, 1)]

def basis_blocks(stamp_basis):
    side = stamp_basis.shape[1] // 2
    padded_basis = jnp.pad(stamp_basis, ((0, 0), (side, side), (side, side)))
    pieces = []
    for row_step, col_step in tap_list():
        top = side + side // 2 - side * row_step
        left = side + side // 2 - side * col_step
        pieces.append(padded_basis[:, top:top + side, left:left + side])
    return jnp.stack(pieces)

def render(padded_amp, blocks, dimple_rows, dimple_cols):
    side = blocks.shape[2]
    shifted = jnp.stack([padded_amp[:, 1 + r:1 + r + dimple_rows, 1 + c:1 + c + dimple_cols] for r, c in tap_list()])
    tiles = jnp.einsum('tpab,tpyx->aybx', shifted, blocks, precision=lax.Precision.HIGHEST)
    return tiles.reshape(dimple_rows * side, dimple_cols * side)

def render_back(padded_grad, blocks, dimple_rows, dimple_cols):
    side = blocks.shape[2]
    framed = padded_grad.reshape(dimple_rows + 2, side, dimple_cols + 2, side)
    summed = jnp.zeros((blocks.shape[1], dimple_rows, dimple_cols), jnp.float32)
    for index, (r, c) in enumerate(tap_list()):
        window = framed[1 - r:1 - r + dimple_rows, :, 1 - c:1 - c + dimple_cols, :]
        summed = summed + jnp.einsum('aybx,pyx->pab', window, blocks[index], precision=lax.Precision.HIGHEST)
    return summed

def conv_forward(padded, weight, bias, dilate, out_rows, out_cols):
    channels = weight.shape[1]
    summed = jnp.zeros((channels, out_rows, out_cols), jnp.float32)
    zero = jnp.asarray(0, jnp.int32)
    for index, (r, c) in enumerate(tap_list()):
        window = lax.dynamic_slice(padded, (zero, (DMAX + r * dilate).astype(jnp.int32), (DMAX + c * dilate).astype(jnp.int32)), (channels, out_rows, out_cols))
        summed = summed + jnp.einsum('oc,chw->ohw', weight[index].astype(jnp.float32), window.astype(jnp.float32), precision=lax.Precision.HIGHEST)
    return summed + bias[:, None, None]

def conv_back(padded, weight, dilate, out_rows, out_cols):
    channels = weight.shape[1]
    summed = jnp.zeros((channels, out_rows, out_cols), jnp.float32)
    zero = jnp.asarray(0, jnp.int32)
    for index, (r, c) in enumerate(tap_list()):
        window = lax.dynamic_slice(padded, (zero, (DMAX - r * dilate).astype(jnp.int32), (DMAX - c * dilate).astype(jnp.int32)), (channels, out_rows, out_cols))
        summed = summed + jnp.einsum('oc,ohw->chw', weight[index].astype(jnp.float32), window.astype(jnp.float32), precision=lax.Precision.HIGHEST)
    return summed

def silu_slope(value):
    logistic = jax.nn.sigmoid(value)
    return logistic * (1.0 + value * (1.0 - logistic))

def reference(design, active, stamp_basis, film_field, lift_weight, lift_bias, conv_weight, conv_bias, readout, target, dilation):
    blocks = basis_blocks(stamp_basis)
    active_mask = active.astype(jnp.float32)
    cell_rows, cell_cols = target.shape
    params = design
    objectives = []
    for iteration in range(ITERS):
        amplitude = params * active_mask
        padded_amp = jnp.pad(amplitude, ((0, 0), (1, 1), (1, 1)))
        height = render(padded_amp, blocks, GR, GC)
        state = (lift_weight[:, None, None] * height[None] + lift_bias[:, None, None] + film_field.astype(jnp.float32)).astype(jnp.bfloat16)
        pres = []
        for layer in range(LAYERS):
            padded = jnp.pad(state, ((0, 0), (DMAX, DMAX), (DMAX, DMAX)))
            pre = conv_forward(padded, conv_weight[layer], conv_bias[layer], dilation[layer], cell_rows, cell_cols)
            pres.append(pre)
            state = (state.astype(jnp.float32) + jax.nn.silu(pre)).astype(jnp.bfloat16)
        pressure = lax.optimization_barrier(jnp.sum(readout[:, None, None] * state.astype(jnp.float32), axis=0))
        misfit = pressure - target
        objectives.append(0.5 * jnp.mean(misfit * misfit))
        adjoint = readout[:, None, None] * (misfit / (STRIDE * STRIDE))[None]
        for layer in range(LAYERS - 1, -1, -1):
            slope = (adjoint * silu_slope(pres[layer])).astype(jnp.bfloat16)
            padded = jnp.pad(slope, ((0, 0), (DMAX, DMAX), (DMAX, DMAX)))
            adjoint = adjoint + conv_back(padded, conv_weight[layer], dilation[layer], cell_rows, cell_cols)
        height_grad = lax.optimization_barrier(jnp.sum(lift_weight[:, None, None] * adjoint, axis=0))
        gradient = render_back(jnp.pad(height_grad, STRIDE), blocks, GR, GC) * active_mask
        mean_square = jnp.sum(gradient * gradient) / (NPARAM * GR * GC)
        params = params - step_rate * gradient / jnp.sqrt(mean_square + norm_eps)
    return (params, jnp.stack(objectives))
```

```python
import functools

import jax
import jax.numpy as jnp
import numpy as np
from jax import lax
from jax.experimental import pallas as pl
from jax.experimental.pallas import tpu as pltpu
from jax.sharding import PartitionSpec as P

f32 = jnp.float32
bf16 = jnp.bfloat16
step_rate = 0.25
norm_eps = 1e-06

NP = 6
LAYERS = 4
SIDE = 16
HALF = 8
TR = 32
TC = 128
HALO = 64
WIDE = TC + 2 * HALO
ROWS = TR + 2 * HALO
VMEM_LIMIT = 56 * 1024 * 1024


def iota(shape, dim):
    return lax.broadcasted_iota(jnp.int32, shape, dim)


def split3(x):
    hi = x.astype(bf16)
    rest = x - hi.astype(f32)
    mid = rest.astype(bf16)
    low = (rest - mid.astype(f32)).astype(bf16)
    return hi, mid, low


def dot(a, b):
    return jnp.dot(a, b, preferred_element_type=f32)


def exact_dot(x, ones):
    hi, mid, low = split3(x)
    return dot(hi, ones) + dot(mid, ones) + dot(low, ones)


def lane_fields(width):
    lane = iota((1, width), 1) % 128
    group = lane // 10
    return group, lane - 10 * group, lane < 120


def pack_kernel(film_ref, design_ref, active_ref, target_ref, own_ref, right_ref, left_ref):
    low_half = iota((16, TC), 1) < HALO
    group, spot, used = lane_fields(TC)
    spread = jnp.where(
        (iota((HALF, TC), 0) == spot - 1) & used, 1.0, 0.0
    ).astype(bf16)
    active = active_ref[...].astype(f32)
    row_of = iota((2, TC), 0)
    amp_row = jnp.zeros((1, TC), f32)
    act_row = jnp.zeros((1, TC), f32)
    act_spread = exact_dot(active, spread)
    for p in range(NP):
        mine = row_of + 2 * p == group
        placed = jnp.where(mine, exact_dot(design_ref[p] * active, spread), 0.0)
        amp_row = amp_row + jnp.sum(placed, axis=0, keepdims=True)
        act_row = act_row + jnp.sum(jnp.where(mine, act_spread, 0.0), axis=0, keepdims=True)
    hi, mid, low = split3(amp_row)
    sub = iota((16, TC), 0)
    tile = jnp.where(sub == 0, hi.astype(f32), 0.0)
    tile = jnp.where(sub == 1, mid.astype(f32), tile)
    tile = jnp.where(sub == 2, low.astype(f32), tile)
    tile = jnp.where(sub == 3, act_row, tile).astype(bf16)
    own_ref[0] = tile
    right_ref[19] = tile
    left_ref[19] = tile
    film = jnp.swapaxes(film_ref[...].astype(f32), 0, 1)
    rows = [film[r] for r in range(TR)]
    for piece in split3(target_ref[...]):
        wide = piece.astype(f32)
        rows += [wide[:16], wide[16:]]
    for r, row in enumerate(rows):
        own_ref[1 + r] = row.astype(bf16)
    for r in range(19):
        a, b = rows[r], rows[r + 19]
        right_ref[r] = jnp.where(low_half, pltpu.roll(a, HALO, 1), b).astype(bf16)
        left_ref[r] = jnp.where(low_half, a, pltpu.roll(b, HALO, 1)).astype(bf16)


def widen_kernel(own_ref, from_left_ref, from_right_ref, one_ref, two_ref, three_ref):
    low_half = iota((16, TC), 1) < HALO
    zero = jnp.zeros((16, TC), bf16)
    for out_ref in (one_ref, two_ref, three_ref):
        out_ref[0, :, :TC] = from_left_ref[19]
        out_ref[0, :, TC:] = own_ref[0]
        out_ref[1, :, :TC] = from_right_ref[19]
        out_ref[1, :, TC:] = zero
    for r in range(38):
        own = pltpu.roll(own_ref[1 + r].astype(f32), HALO, 1)
        if r < 19:
            left = from_left_ref[r].astype(f32)
            right = pltpu.roll(from_right_ref[r].astype(f32), HALO, 1)
        else:
            left = pltpu.roll(from_left_ref[r - 19].astype(f32), HALO, 1)
            right = from_right_ref[r - 19].astype(f32)
        first = jnp.where(low_half, left, own).astype(bf16)
        second = jnp.where(low_half, own, right).astype(bf16)
        one_ref[2 + r, :, :TC] = first
        one_ref[2 + r, :, TC:] = second
        if r < TR:
            two_ref[2 + r, :, :TC] = first
            two_ref[2 + r, :, TC:] = second


def combine(gathered):
    own, ring = gathered[:, :128], gathered[:, 128:]
    group, spot, used = lane_fields(128)
    top = (group % 2 == 0) & used
    bottom = (group % 2 == 1) & used
    zero = jnp.zeros((16, 128), f32)
    above = jnp.concatenate([zero, ring[:240]], axis=0)
    below = jnp.concatenate([ring[16:], zero], axis=0)
    summed = own + jnp.where(top, above, 0.0) + jnp.where(bottom, below, 0.0)
    place = iota((256, 128), 0) % 16
    left = jnp.where(place == 0, 0.0, pltpu.roll(summed, 1, 0))
    right = jnp.where(place == 15, 0.0, pltpu.roll(summed, 255, 0))
    left = pltpu.roll(left, 120, 1)
    right = pltpu.roll(right, 8, 1)
    whole = summed + jnp.where(spot == 1, left, 0.0) + jnp.where(spot == 8, right, 0.0)
    whole = jnp.where((spot >= 1) & (spot <= 8) & used, whole, 0.0)
    squares = jnp.sum(jnp.sum(whole * whole, axis=0, keepdims=True), axis=1, keepdims=True)
    lane = iota((1, 128), 1)
    misfits = jnp.sum(
        jnp.where(lane == 120, jnp.sum(own, axis=0, keepdims=True), 0.0), axis=1, keepdims=True
    )
    return whole, squares, misfits


def rate_of(squares, entries):
    return step_rate / jnp.sqrt(squares / entries + norm_eps)


def step_kernel(second, grid, *refs):
    row_count, col_count = grid
    if second:
        (place_ref, dil_ref, vec_ref, wf_ref, wb_ref, stamp_ref, own_ref, u1_ref, u2_ref, u3_ref,
         d1_ref, d2_ref, d3_ref, gathered_ref, out_ref, moved_ref, cat0_ref, cat1_ref, sp_ref, adj_ref,
         height_ref, hg_ref, s2_ref, ampx_ref, acc_ref, whole_ref) = refs
    else:
        (place_ref, dil_ref, vec_ref, wf_ref, wb_ref, stamp_ref, own_ref, u1_ref, u2_ref, u3_ref,
         d1_ref, d2_ref, d3_ref, out_ref, cat0_ref, cat1_ref, sp_ref, adj_ref,
         height_ref, hg_ref, s2_ref, ampx_ref, acc_ref) = refs
    my_row = place_ref[0]
    my_col = place_ref[1]
    group, spot, used = lane_fields(128)
    by_row = [u3_ref, u2_ref, u1_ref, own_ref, d1_ref, d2_ref, d3_ref]

    for k in range(2):
        pick = jnp.where(
            iota((32, WIDE), 0) == (iota((32, WIDE), 1) + HALF) % SIDE + SIDE * k, 1.0, 0.0
        ).astype(bf16)
        s2_ref[k] = exact_dot(stamp_ref[...], pick)

    if second:
        whole, squares, _ = combine(gathered_ref[...])
        whole_ref[...] = whole
        rate = rate_of(squares, float(row_count * col_count * NP * 16))
    masks = iota((16, 384), 0) == jnp.concatenate([group] * 3, axis=1)
    acts = {}
    stacked = []
    for dr in range(-3, 4):
        ref = by_row[dr + 3]
        tiles = [ref[0, :, :TC], ref[0, :, TC:], ref[1, :, :TC]]
        pieces = []
        for dc, tile in zip((-1, 0, 1), tiles):
            t = tile.astype(f32)
            amp = t[0:1] + t[1:2] + t[2:3]
            if second:
                r, c = my_row + dr, my_col + dc
                inside = (r >= 0) & (r < row_count) & (c >= 0) & (c < col_count)
                dev = jnp.where(inside, r * col_count + c, 0)
                moved = rate * whole_ref[pl.ds(dev, 1), :]
                moved = moved * jnp.where(inside, 1.0, 0.0)
                if dr == 0 and dc == 0:
                    moved_ref[...] = moved
                amp = amp - moved
            pieces.append(amp)
            acts[dr, dc] = t[3:4]
        row = jnp.concatenate(pieces, axis=1)
        stacked.append(jnp.where(masks, row, 0.0))
    stacked = jnp.concatenate(stacked, axis=0)
    lane3 = iota((384, WIDE), 0)
    lane1 = lane3 % 128
    spot3 = lane1 % 10
    for k in range(2):
        b = (iota((384, WIDE), 1) + HALF) // SIDE - HALO // SIDE - k
        hit = (b == HALF * (lane3 // 128 - 1) + spot3 - 1) & (spot3 >= 1) & (spot3 <= 8)
        expand = jnp.where(hit & (lane1 < 120), 1.0, 0.0).astype(bf16)
        ampx_ref[k] = exact_dot(stacked, expand)

    for a in range(-4, 6):
        for half in range(2):
            if half == 0:
                terms = ((a, 8), (a - 1, 24))
            else:
                terms = ((a, 16), (a + 1, 0))
            total = jnp.zeros((HALF, WIDE), f32)
            for dimple, first in terms:
                dr, i = dimple // 2, dimple % 2
                for p in range(NP):
                    for k in range(2):
                        row = 16 * (dr + 3) + 2 * p + i
                        total = total + (
                            s2_ref[k, 32 * p + first : 32 * p + first + HALF, :]
                            * ampx_ref[k, row : row + 1, :]
                        )
            start = HALO + SIDE * a + HALF * half
            height_ref[start : start + HALF, :] = total

    col = my_col * TC + iota((16, WIDE), 1) - HALO
    in_map = (col >= 0) & (col < col_count * TC)

    cats = (cat0_ref, cat1_ref)

    def put(slot, b, value, shift):
        cat = cats[slot]
        value = jnp.where(in_map, value, 0.0)
        cat[b, 16:32, :] = value.astype(bf16)
        cat[b, 0:16, :] = pltpu.roll(value, shift, 1).astype(bf16)
        cat[b, 32:48, :] = pltpu.roll(value, WIDE - shift, 1).astype(bf16)

    def wide_row(ref):
        return jnp.broadcast_to(ref, (16, WIDE))

    lift_w = wide_row(vec_ref[0])
    map_lo = jnp.maximum(0, HALO - my_row * TR)
    map_hi = jnp.minimum(ROWS, HALO + (row_count - my_row) * TR)
    d = [dil_ref[l] for l in range(LAYERS)]
    total_d = d[0] + d[1] + d[2] + d[3]

    def round_up(x):
        return (x + 7) // 8 * 8

    def bounds(reach):
        wide = round_up(reach)
        return jnp.maximum(map_lo, HALO - wide), jnp.minimum(map_hi, HALO + TR + wide)

    def over(lo, hi, some_rows):
        count = hi - lo

        def body(step, _):
            some_rows(lo + 32 * step, 32)
            return 0

        full = count // 32
        lax.fori_loop(0, full, body, 0)
        rest = count - 32 * full
        half = rest // 16

        @pl.when(half > 0)
        def _():
            some_rows(lo + 32 * full, 16)

        @pl.when(rest - 16 * half > 0)
        def _():
            some_rows(hi - 8, 8)

    lo0, hi0 = bounds(2 * total_d)
    lift_b = wide_row(vec_ref[1])
    for n, ref in enumerate((u2_ref, u1_ref, own_ref, d1_ref, d2_ref)):
        here = my_row + n - 2
        valid = (here >= 0) & (here < row_count)
        first = jnp.clip(lo0 - n * TR, 0, TR)
        after = jnp.clip(hi0 - n * TR, 0, TR)

        def rows(step, _):
            r0 = first + step * 8
            hs = [height_ref[pl.ds(n * TR + r0 + q, 1), :] for q in range(8)]
            for q in range(8):
                film = ref[2 + r0 + q].astype(f32)
                value = (lift_w * hs[q] + lift_b + film).astype(bf16).astype(f32)
                put(0, n * TR + r0 + q, value, d[0])
            return 0

        lax.fori_loop(0, (after - first) // 8, rows, 0)

        @pl.when(jnp.logical_not(valid))
        def _():
            def blank(r, _):
                cat0_ref[n * TR + r] = jnp.zeros((48, WIDE), bf16)
                cat1_ref[n * TR + r] = jnp.zeros((48, WIDE), bf16)
                return 0

            lax.fori_loop(0, TR, blank, 0)

    def convs(w, slot, b0, n, dil):
        cat = cats[slot]
        out = []
        for q in range(n):
            b = b0 + q
            out.append(dot(w, jnp.concatenate([cat[b - dil], cat[b], cat[b + dil]], axis=0)))
        return out

    def parts(pre):
        s = 0.5 + 0.5 * jnp.tanh(0.5 * pre)
        silu = pre * s
        return silu, s + silu * (1.0 - s)

    reach = 2 * total_d
    for l in range(LAYERS - 1):
        slot = l % 2
        w = wf_ref[l]
        bias = wide_row(vec_ref[3 + l])
        reach = reach - d[l]
        lo, hi = bounds(reach)

        def forward(b0, n):
            pres = convs(w, slot, b0, n, d[l])
            for q in range(n):
                b = b0 + q
                silu, slope = parts(pres[q] + bias)
                sp_ref[l, b] = slope
                value = cats[slot][b, 16:32, :].astype(f32) + silu
                put(1 - slot, b, value.astype(bf16).astype(f32), d[l + 1])

        over(lo, hi, forward)

    for n, ref in enumerate((u1_ref, own_ref, d1_ref)):
        target = ref[34:36].astype(f32) + ref[36:38].astype(f32) + ref[38:40].astype(f32)
        height_ref[TR * (n + 1) : TR * (n + 1) + 16, :] = target[0]
        height_ref[TR * (n + 1) + 16 : TR * (n + 2), :] = target[1]

    acc_ref[...] = jnp.zeros_like(acc_ref)
    lo, hi = bounds(total_d)
    w3 = wf_ref[3]
    bias3 = wide_row(vec_ref[6])
    readout = wide_row(vec_ref[2])

    def turn(b0, n):
        pres = convs(w3, 1, b0, n, d[3])
        targets = [height_ref[pl.ds(b0 + q, 1), :] for q in range(n)]
        for q in range(n):
            b = b0 + q
            silu, slope = parts(pres[q] + bias3)
            value = (cat1_ref[b, 16:32, :].astype(f32) + silu).astype(bf16).astype(f32)
            pressure = jnp.sum(readout * value, axis=0, keepdims=True)
            misfit = pressure - targets[q]
            acc_ref[pl.ds(b, 1), :] = misfit * misfit
            adj = readout * (misfit * (1.0 / (SIDE * SIDE)))
            adj_ref[b] = adj
            put(0, b, (adj * slope).astype(bf16).astype(f32), d[3])

    over(lo, hi, turn)

    reach = total_d
    for l in range(LAYERS - 1, 0, -1):
        slot = (l + 1) % 2
        wb = wb_ref[l]
        reach = reach - d[l]
        lo, hi = bounds(reach)

        def backward(b0, n):
            sums = convs(wb, slot, b0, n, d[l])
            olds = [adj_ref[b0 + q] for q in range(n)]
            for q in range(n):
                b = b0 + q
                adj = olds[q] + sums[q]
                adj_ref[b] = adj
                put(1 - slot, b, (adj * sp_ref[l - 1, b]).astype(bf16).astype(f32), d[l - 1])

        over(lo, hi, backward)

    w0 = wb_ref[0]
    sums = convs(w0, 1, HALO, TR, d[0])
    for q in range(TR):
        adj = adj_ref[HALO + q] + sums[q]
        hg_ref[q : q + 1, :] = jnp.sum(lift_w * adj, axis=0, keepdims=True)

    hg = pltpu.roll(hg_ref[...], WIDE - HALO, 1)[:, :TC]
    spans = {-1: (0, 8, 24), 0: (0, 24, 8), 1: (8, 32, 0), 2: (24, 32, 0)}
    message = []
    for block in ((0, 1), (2, -1)):
        lanes = jnp.zeros((1, TC), f32)
        for k in range(2):
            rows = []
            for p in range(NP):
                for dimple in block:
                    lo_r, hi_r, first = spans[dimple]
                    n = hi_r - lo_r
                    prod = hg[lo_r:hi_r] * s2_ref[k, 32 * p + first : 32 * p + first + n, :TC]
                    rows.append(jnp.sum(prod, axis=0, keepdims=True))
            rows += [jnp.zeros((4, TC), f32)]
            sums = jnp.concatenate(rows, axis=0)
            c = iota((TC, TC), 0)
            gather = jnp.where(((c + HALF) // SIDE - k + 1 == spot) & used, 1.0, 0.0)
            z = exact_dot(sums, gather.astype(bf16))
            lanes = lanes + jnp.sum(
                jnp.where(iota((16, TC), 0) == group, z, 0.0), axis=0, keepdims=True
            )
        message.append(lanes)

    def act_ext(dr):
        act = acts[dr, 0]
        act = act + jnp.where(spot == 0, pltpu.roll(acts[dr, -1], 120, 1), 0.0)
        return act + jnp.where(spot == 9, pltpu.roll(acts[dr, 1], 8, 1), 0.0)

    lane = iota((1, TC), 1)
    own_act = act_ext(0)
    ring_act = jnp.where(group % 2 == 0, act_ext(1), act_ext(-1))
    acc = jnp.sum(acc_ref[HALO : HALO + TR, :], axis=0, keepdims=True)
    inner = (iota((1, WIDE), 1) >= HALO) & (iota((1, WIDE), 1) < HALO + TC)
    local = 0.5 * jnp.sum(jnp.where(inner, acc, 0.0), axis=1, keepdims=True)
    first = jnp.where(used, message[0] * own_act, jnp.where(lane == 120, local, 0.0))
    ring = jnp.where(used, message[1] * ring_act, 0.0)
    out_ref[:, :TC] = first
    out_ref[:, TC:] = ring


def final_kernel(grid, place_ref, design_ref, gathered1_ref, gathered2_ref, moved_ref, new_ref, obj_ref, whole_ref):
    row_count, col_count = grid
    whole, squares, misfit2 = combine(gathered2_ref[...])
    lane = iota((1, 128), 1)
    own = jnp.sum(gathered1_ref[:, :128], axis=0, keepdims=True)
    misfit1 = jnp.sum(jnp.where(lane == 120, own, 0.0), axis=1, keepdims=True)
    whole_ref[...] = whole
    entries = float(row_count * col_count * NP * 16)
    cells = float(row_count * col_count * TR * TC)
    dev = place_ref[0] * col_count + place_ref[1]
    moved = moved_ref[...] + rate_of(squares, entries) * whole_ref[pl.ds(dev, 1), :]
    group, _, _ = lane_fields(128)
    by_group = jnp.where(iota((16, 128), 0) == group, moved, 0.0)
    lanes = iota((128, HALF), 0)
    pick = jnp.where((lanes % 10 == iota((128, HALF), 1) + 1) & (lanes < 120), 1.0, 0.0)
    change = exact_dot(by_group, pick.astype(bf16))
    for p in range(NP):
        new_ref[p] = design_ref[p] - change[2 * p : 2 * p + 2]
    obj_ref[...] = jnp.where(iota((1, 128), 1) == 0, misfit1, misfit2) / cells


def vmem():
    return pl.BlockSpec(memory_space=pltpu.VMEM)


def smem():
    return pl.BlockSpec(memory_space=pltpu.SMEM)


def shape(dims, kind):
    return jax.ShapeDtypeStruct(dims, kind)


def params():
    return pltpu.CompilerParams(vmem_limit_bytes=VMEM_LIMIT)


def on_device(
    row_count, col_count, design, active, stamp_basis, film_field, lift_weight, lift_bias,
    conv_weight, conv_bias, readout, target, dilation,
):
    grid = (row_count, col_count)
    place = jnp.stack([lax.axis_index("rows"), lax.axis_index("cols")]).astype(jnp.int32)
    own, to_right, to_left = pl.pallas_call(
        pack_kernel,
        out_shape=(shape((39, 16, TC), bf16), shape((20, 16, TC), bf16), shape((20, 16, TC), bf16)),
        in_specs=[vmem()] * 4,
        out_specs=(vmem(),) * 3,
        compiler_params=params(),
        name="pack",
    )(film_field, design, active, target)

    def shifted(x, axis, by):
        count = lax.axis_size(axis)
        return lax.ppermute(x, axis, [(i, i + by) for i in range(count) if 0 <= i + by < count])

    from_left = shifted(to_right, "cols", 1)
    from_right = shifted(to_left, "cols", -1)
    one, two, three = pl.pallas_call(
        widen_kernel,
        out_shape=(shape((40, 16, WIDE), bf16), shape((34, 16, WIDE), bf16), shape((2, 16, WIDE), bf16)),
        in_specs=[vmem()] * 3,
        out_specs=(vmem(),) * 3,
        compiler_params=params(),
        name="widen",
    )(own, from_left, from_right)
    u1, d1 = shifted(one, "rows", 1), shifted(one, "rows", -1)
    u2, d2 = shifted(two, "rows", 2), shifted(two, "rows", -2)
    u3, d3 = shifted(three, "rows", 3), shifted(three, "rows", -3)

    wf = jnp.transpose(conv_weight, (0, 2, 1, 3)).reshape(LAYERS, 16, 144)
    wb = jnp.transpose(conv_weight[:, ::-1], (0, 3, 1, 2)).reshape(LAYERS, 16, 144)
    vec = jnp.concatenate(
        [lift_weight[None], lift_bias[None], readout[None], conv_bias], axis=0
    )[:, :, None]
    stamp = stamp_basis.reshape(NP * 32, 32)
    scratch = [
        pltpu.VMEM((ROWS, 48, WIDE), bf16),
        pltpu.VMEM((ROWS, 48, WIDE), bf16),
        pltpu.VMEM((LAYERS - 1, ROWS, 16, WIDE), f32),
        pltpu.VMEM((ROWS, 16, WIDE), f32),
        pltpu.VMEM((ROWS, WIDE), f32),
        pltpu.VMEM((TR, WIDE), f32),
        pltpu.VMEM((2, NP * 32, WIDE), f32),
        pltpu.VMEM((2, 112, WIDE), f32),
        pltpu.VMEM((ROWS, WIDE), f32),
    ]
    common = (place, dilation, vec, wf, wb, stamp, one, u1, u2, u3, d1, d2, d3)
    specs = [smem(), smem()] + [vmem()] * 11

    def gather(message):
        n = row_count * col_count
        spread = jnp.broadcast_to(message[None], (n, 1, 2 * TC))
        return lax.all_to_all(spread, ("rows", "cols"), 0, 0).reshape(n, 2 * TC)

    message1 = pl.pallas_call(
        functools.partial(step_kernel, False, grid),
        out_shape=shape((1, 2 * TC), f32),
        in_specs=specs,
        out_specs=vmem(),
        scratch_shapes=scratch,
        compiler_params=params(),
        name="step_one",
    )(*common)
    gathered1 = gather(message1)
    message2, moved = pl.pallas_call(
        functools.partial(step_kernel, True, grid),
        out_shape=(shape((1, 2 * TC), f32), shape((1, TC), f32)),
        in_specs=specs + [vmem()],
        out_specs=(vmem(), vmem()),
        scratch_shapes=scratch + [pltpu.VMEM((row_count * col_count, TC), f32)],
        compiler_params=params(),
        name="step_two",
    )(*common, gathered1)
    gathered2 = gather(message2)
    new_design, objective = pl.pallas_call(
        functools.partial(final_kernel, grid),
        out_shape=(shape((NP, 2, HALF), f32), shape((1, TC), f32)),
        in_specs=[smem()] + [vmem()] * 4,
        out_specs=(vmem(), vmem()),
        scratch_shapes=[pltpu.VMEM((row_count * col_count, TC), f32)],
        compiler_params=params(),
        name="finish",
    )(place, design, gathered1, gathered2, moved)
    return new_design, objective[0, :2]


def solution(mesh):
    placed = (
        P(None, "rows", "cols"),
        P("rows", "cols"),
        P(),
        P(None, "rows", "cols"),
        P(),
        P(),
        P(),
        P(),
        P(),
        P("rows", "cols"),
        P(),
    )
    return jax.shard_map(
        functools.partial(on_device, mesh.shape["rows"], mesh.shape["cols"]),
        mesh=mesh,
        in_specs=placed,
        out_specs=(P(None, "rows", "cols"), P()),
        check_vma=False,
    )
```

```python
import functools

import jax
import jax.numpy as jnp
import numpy as np
from jax import lax
from jax.experimental import pallas as pl
from jax.experimental.pallas import tpu as pltpu
from jax.sharding import PartitionSpec as P

f32 = jnp.float32
bf16 = jnp.bfloat16
step_rate = 0.25
norm_eps = 1e-06

NP = 6
LAYERS = 4
SIDE = 16
HALF = 8
TR = 32
TC = 128
HALO = 64
WIDE = TC + 2 * HALO
ROWS = TR + 2 * HALO
SPARE = ROWS + 16
PAIRS = 16
MIB = 1024 * 1024


def iota(shape, dim):
    return lax.broadcasted_iota(jnp.int32, shape, dim)


def cell_col(dims):
    lane = iota(dims, 1)
    return jnp.where(lane < TC + HALO, lane, lane - WIDE)


def split3(x):
    hi = x.astype(bf16)
    rest = x - hi.astype(f32)
    mid = rest.astype(bf16)
    low = (rest - mid.astype(f32)).astype(bf16)
    return hi, mid, low


def dot(a, b):
    return jnp.dot(a, b, preferred_element_type=f32)


def exact_dot(x, ones):
    hi, mid, low = split3(x)
    return dot(hi, ones) + dot(mid, ones) + dot(low, ones)


def lane_fields(width):
    lane = iota((1, width), 1) % 128
    group = lane // 10
    return group, lane - 10 * group, lane < 120


def pack_kernel(film_ref, design_ref, active_ref, target_ref, one_ref, up_ref, down_ref):
    group, spot, used = lane_fields(TC)
    spread = jnp.where(
        (iota((HALF, TC), 0) == spot - 1) & used, 1.0, 0.0
    ).astype(bf16)
    active = active_ref[...].astype(f32)
    row_of = iota((2, TC), 0)
    amp_row = jnp.zeros((1, TC), f32)
    act_row = jnp.zeros((1, TC), f32)
    act_spread = exact_dot(active, spread)
    for p in range(NP):
        mine = row_of + 2 * p == group
        placed = jnp.where(mine, exact_dot(design_ref[p] * active, spread), 0.0)
        amp_row = amp_row + jnp.sum(placed, axis=0, keepdims=True)
        act_row = act_row + jnp.sum(jnp.where(mine, act_spread, 0.0), axis=0, keepdims=True)
    hi, mid, low = split3(amp_row)
    sub = iota((16, TC), 0)
    tile = jnp.where(sub == 0, hi.astype(f32), 0.0)
    tile = jnp.where(sub == 1, mid.astype(f32), tile)
    tile = jnp.where(sub == 2, low.astype(f32), tile)
    tile = jnp.where(sub == 3, act_row, tile).astype(bf16)
    one_ref[0] = tile
    up_ref[0] = tile
    down_ref[0] = tile
    film = jnp.swapaxes(film_ref[...].astype(f32), 0, 1).astype(bf16)
    one_ref[1 : 1 + TR] = film
    up_ref[1 : 1 + TR] = film
    down_ref[1 : 1 + TR] = film
    for n, piece in enumerate(split3(target_ref[...])):
        one_ref[33 + 2 * n] = piece[:16]
        one_ref[34 + 2 * n] = piece[16:]


SIDES = 96
AMPS = 89


def tile_pairs(u2, u1, own, d1, d2):
    pairs = [((u2, 1 + r), (u1, 1 + r)) for r in range(TR)]
    pairs += [((own, 1 + r), (own, 17 + r)) for r in range(16)]
    pairs += [((d1, 1 + r), (d2, 1 + r)) for r in range(TR)]
    pairs += [((u1, 33 + r), (d1, 33 + r)) for r in range(6)]
    return pairs + [((own, 33 + r), (own, 36 + r)) for r in range(3)]


def amp_tiles(u2, u1, own, d1, d2):
    return ((u2, 33), (u2, 0), (u1, 0), (own, 0), (d1, 0), (d2, 0), (d2, 33))


def swap_halves(x):
    return pltpu.roll(x, TC // 2, 1)


def halve_kernel(own_ref, u1_ref, u2_ref, d1_ref, d2_ref, right_ref, left_ref):
    low_half = iota((16, TC), 1) < HALO
    pairs = tile_pairs(u2_ref, u1_ref, own_ref, d1_ref, d2_ref)
    for n, ((ref_a, a), (ref_b, b)) in enumerate(pairs):
        first, second = ref_a[a].astype(f32), ref_b[b].astype(f32)
        right_ref[n] = jnp.where(low_half, swap_halves(first), second).astype(bf16)
        left_ref[n] = jnp.where(low_half, first, swap_halves(second)).astype(bf16)
    for n, (ref, at) in enumerate(amp_tiles(u2_ref, u1_ref, own_ref, d1_ref, d2_ref)):
        right_ref[AMPS + n] = ref[at]
        left_ref[AMPS + n] = ref[at]


def combine(gathered):
    own, ring = gathered[:, :128], gathered[:, 128:]
    group, spot, used = lane_fields(128)
    top = (group % 2 == 0) & used
    bottom = (group % 2 == 1) & used
    zero = jnp.zeros((16, 128), f32)
    above = jnp.concatenate([zero, ring[:240]], axis=0)
    below = jnp.concatenate([ring[16:], zero], axis=0)
    summed = own + jnp.where(top, above, 0.0) + jnp.where(bottom, below, 0.0)
    place = iota((256, 128), 0) % 16
    left = jnp.where(place == 0, 0.0, pltpu.roll(summed, 1, 0))
    right = jnp.where(place == 15, 0.0, pltpu.roll(summed, 255, 0))
    left = pltpu.roll(left, 120, 1)
    right = pltpu.roll(right, 8, 1)
    whole = summed + jnp.where(spot == 1, left, 0.0) + jnp.where(spot == 8, right, 0.0)
    whole = jnp.where((spot >= 1) & (spot <= 8) & used, whole, 0.0)
    squares = jnp.sum(jnp.sum(whole * whole, axis=0, keepdims=True), axis=1, keepdims=True)
    lane = iota((1, 128), 1)
    misfits = jnp.sum(
        jnp.where(lane == 120, jnp.sum(own, axis=0, keepdims=True), 0.0), axis=1, keepdims=True
    )
    return whole, squares, misfits


def rate_of(squares, entries):
    return step_rate / jnp.sqrt(squares / entries + norm_eps)


def prep_kernel(stamp_ref, s2_ref, expand_ref):
    for k in range(2):
        pick = jnp.where(
            iota((32, WIDE), 0) == (iota((32, WIDE), 1) + HALF) % SIDE + SIDE * k, 1.0, 0.0
        ).astype(bf16)
        s2_ref[k] = exact_dot(stamp_ref[...], pick)
    lane3 = iota((384, WIDE), 0)
    lane1 = lane3 % 128
    spot3 = lane1 % 10
    for k in range(2):
        b = (cell_col((384, WIDE)) + HALO + HALF) // SIDE - HALO // SIDE - k
        hit = (b == HALF * (lane3 // 128 - 1) + spot3 - 1) & (spot3 >= 1) & (spot3 <= 8)
        expand_ref[k] = jnp.where(hit & (lane1 < 120), 1.0, 0.0).astype(bf16)


def step_kernel(second, grid, *refs):
    row_count, col_count = grid
    (place_ref, dil_ref, vec_ref, wf_ref, wb_ref, s2_ref, expand_ref, own_ref, u1_ref, u2_ref, d1_ref,
     d2_ref, from_left_ref, from_right_ref) = refs[:14]
    rest = refs[14:]
    if second:
        gathered_ref, out_ref, moved_ref, whole_ref = rest[:4]
        rest = rest[4:]
    else:
        out_ref, rest = rest[0], rest[1:]
    cat0_ref, cat1_ref, sp_ref, adj_ref, height_ref, hg_ref, ampx_ref, acc_ref = rest
    my_row = place_ref[0]
    my_col = place_ref[1]
    group, spot, used = lane_fields(128)
    amps = amp_tiles(u2_ref, u1_ref, own_ref, d1_ref, d2_ref)

    if second:
        whole, squares, misfits = combine(gathered_ref[...].reshape(row_count * col_count, 2 * TC))
        whole_ref[...] = whole
        rate = rate_of(squares, float(row_count * col_count * NP * 16))
    masks = iota((16, 384), 0) == jnp.concatenate([group] * 3, axis=1)
    acts = {}
    stacked = []
    for dr in range(-3, 4):
        ref, at = amps[dr + 3]
        tiles = [from_left_ref[AMPS + dr + 3], ref[at], from_right_ref[AMPS + dr + 3]]
        pieces = []
        for dc, tile in zip((-1, 0, 1), tiles):
            t = tile.astype(f32)
            amp = t[0:1] + t[1:2] + t[2:3]
            if second:
                r, c = my_row + dr, my_col + dc
                inside = (r >= 0) & (r < row_count) & (c >= 0) & (c < col_count)
                dev = jnp.where(inside, r * col_count + c, 0)
                moved = rate * whole_ref[pl.ds(dev, 1), :]
                moved = moved * jnp.where(inside, 1.0, 0.0)
                if dr == 0 and dc == 0:
                    moved_ref[...] = jnp.where(iota((1, TC), 1) == 120, misfits, moved)
                amp = amp - moved
            pieces.append(amp)
            acts[dr, dc] = t[3:4]
        row = jnp.concatenate(pieces, axis=1)
        stacked.append(jnp.where(masks, row, 0.0))
    stacked = jnp.concatenate(stacked, axis=0)
    for k in range(2):
        ampx_ref[k] = exact_dot(stacked, expand_ref[k])

    blocks = range(-4, 6)
    for half in range(2):
        totals = [jnp.zeros((HALF, WIDE), f32) for _ in blocks]
        for step, first in ((0, 16 * half if half else 8), (1 if half else -1, 0 if half else 24)):
            for p in range(NP):
                for k in range(2):
                    stamp = s2_ref[k, 32 * p + first : 32 * p + first + HALF, :]
                    for n, a in enumerate(blocks):
                        dr, i = (a + step) // 2, (a + step) % 2
                        row = 16 * (dr + 3) + 2 * p + i
                        totals[n] = totals[n] + stamp * ampx_ref[k, row : row + 1, :]
        for n, a in enumerate(blocks):
            start = HALO + SIDE * a + HALF * half
            height_ref[start : start + HALF, :] = totals[n]

    col = my_col * TC + cell_col((16, WIDE))
    in_map = (col >= 0) & (col < col_count * TC)

    cats = (cat0_ref, cat1_ref)

    def put(slot, b, value, shift):
        cat = cats[slot]
        b = jnp.where(b < map_hi, b, SPARE)
        value = jnp.where(in_map, value, 0.0)
        cat[b, 16:32, :] = value.astype(bf16)
        cat[b, 0:16, :] = pltpu.roll(value, shift, 1).astype(bf16)
        cat[b, 32:48, :] = pltpu.roll(value, WIDE - shift, 1).astype(bf16)

    def wide_row(ref):
        return jnp.broadcast_to(ref, (16, WIDE))

    lift_w = wide_row(vec_ref[0])
    map_lo = jnp.maximum(0, HALO - my_row * TR)
    map_hi = jnp.minimum(ROWS, HALO + (row_count - my_row) * TR)
    d = [dil_ref[l] for l in range(LAYERS)]
    total_d = d[0] + d[1] + d[2] + d[3]

    def bounds(reach):
        return jnp.maximum(map_lo, HALO - reach), jnp.minimum(map_hi, HALO + TR + reach)

    def over(lo, hi, dil, some_pairs):
        count = hi - lo
        whole = count // (2 * dil)
        pairs = whole * dil + jnp.minimum(dil, count - whole * 2 * dil)

        def some(number, base, i):
            firsts = []
            for _ in range(number):
                firsts.append(base + i)
                wrap = i + 1 >= dil
                next_base = jnp.where(wrap, base + 2 * dil, base)
                next_i = jnp.where(wrap, 0, i + 1)
                inside = next_base + next_i < hi
                base = jnp.where(inside, next_base, base)
                i = jnp.where(inside, next_i, i)
            some_pairs(firsts)
            return base, i

        full = pairs // PAIRS
        rest = pairs - PAIRS * full
        full = full + jnp.where(rest > PAIRS // 2, 1, 0)
        base, i = lax.fori_loop(
            0, full, lambda step, at: some(PAIRS, *at), (lo, jnp.int32(0))
        )

        @pl.when((rest > 0) & (rest <= PAIRS // 2))
        def _():
            some(PAIRS // 2, base, i)

    lo0, hi0 = bounds(2 * total_d)
    lift_b = wide_row(vec_ref[1])
    low_half = iota((16, TC), 1) < HALO

    def beside(place, second_row):
        left = from_left_ref[place].astype(f32)
        right = from_right_ref[place].astype(f32)
        if second_row:
            right = swap_halves(right)
        else:
            left = swap_halves(left)
        return jnp.where(low_half, right, left)

    spans = (
        (0, u2_ref, 0, TR, 0, False),
        (1, u1_ref, 0, TR, 0, True),
        (2, own_ref, 0, 16, 32, False),
        (2, own_ref, 16, 16, 32, True),
        (3, d1_ref, 0, TR, 48, False),
        (4, d2_ref, 0, TR, 48, True),
    )
    for n, ref, row0, count, place, second_row in spans:
        here = my_row + n - 2
        valid = (here >= 0) & (here < row_count)
        start = n * TR + row0
        first = jnp.clip(lo0 - start, 0, count)
        after = jnp.clip(hi0 - start, 0, count)

        def rows(step, _):
            r0 = jnp.minimum(first + step * 16, count - 16)
            hs = [height_ref[pl.ds(start + r0 + q, 1), :] for q in range(16)]
            for q in range(16):
                film = jnp.concatenate(
                    [
                        ref[1 + row0 + r0 + q].astype(f32),
                        beside(place + r0 + q, second_row),
                    ],
                    axis=1,
                )
                value = (lift_w * hs[q] + lift_b + film).astype(bf16).astype(f32)
                put(0, start + r0 + q, value, d[0])
            return 0

        lax.fori_loop(0, (after - first + 15) // 16, rows, 0)

        @pl.when(jnp.logical_not(valid))
        def _():
            def blank(r, _):
                cat0_ref[start + r] = jnp.zeros((48, WIDE), bf16)
                cat1_ref[start + r] = jnp.zeros((48, WIDE), bf16)
                return 0

            lax.fori_loop(0, count, blank, 0)

    def convs(w, slot, firsts, dil):
        cat = cats[slot]
        rows, sums = [], []
        for r in firsts:
            near = [cat[r - dil], cat[r], cat[r + dil], cat[r + 2 * dil]]
            both = dot(w, jnp.concatenate(near, axis=0))
            rows += [r, r + dil]
            sums += [both[:16], both[16:]]
        return rows, sums

    def parts(pre):
        s = 0.5 + 0.5 * jnp.tanh(0.5 * pre)
        silu = pre * s
        return silu, s + silu * (1.0 - s)

    reach = 2 * total_d
    for l in range(LAYERS - 1):
        slot = l % 2
        w = wf_ref[l]
        bias = wide_row(vec_ref[3 + l])
        reach = reach - d[l]
        lo, hi = bounds(reach)

        def forward(firsts):
            for b, pre in zip(*convs(w, slot, firsts, d[l])):
                silu, slope = parts(pre + bias)
                sp_ref[l, b] = slope
                value = cats[slot][b, 16:32, :].astype(f32) + silu
                put(1 - slot, b, value.astype(bf16).astype(f32), d[l + 1])

        over(lo, hi, d[l], forward)

    sides = (
        [(80 + r, False) for r in range(6)],
        [(86 + r % 3, r >= 3) for r in range(6)],
        [(80 + r, True) for r in range(6)],
    )
    for n, ref in enumerate((u1_ref, own_ref, d1_ref)):
        for half in range(2):
            target, side = jnp.zeros((16, TC), f32), jnp.zeros((16, TC), f32)
            for piece in (half, half + 2, half + 4):
                target = target + ref[33 + piece].astype(f32)
                side = side + beside(*sides[n][piece])
            first = TR * (n + 1) + 16 * half
            height_ref[first : first + 16, :TC] = target
            height_ref[first : first + 16, TC:] = side

    acc_ref[...] = jnp.zeros_like(acc_ref)
    lo, hi = bounds(total_d)
    w3 = wf_ref[3]
    bias3 = wide_row(vec_ref[6])
    readout = wide_row(vec_ref[2])

    def turn(firsts):
        rows, pres = convs(w3, 1, firsts, d[3])
        targets = [height_ref[pl.ds(b, 1), :] for b in rows]
        for b, pre, target in zip(rows, pres, targets):
            silu, slope = parts(pre + bias3)
            value = (cat1_ref[b, 16:32, :].astype(f32) + silu).astype(bf16).astype(f32)
            pressure = jnp.sum(readout * value, axis=0, keepdims=True)
            misfit = pressure - target
            acc_ref[pl.ds(b, 1), :] = misfit * misfit
            adj = readout * (misfit * (1.0 / (SIDE * SIDE)))
            adj_ref[b] = adj
            put(0, b, (adj * slope).astype(bf16).astype(f32), d[3])

    over(lo, hi, d[3], turn)

    reach = total_d
    for l in range(LAYERS - 1, 0, -1):
        slot = (l + 1) % 2
        wb = wb_ref[l]
        reach = reach - d[l]
        lo, hi = bounds(reach)

        def backward(firsts):
            rows, sums = convs(wb, slot, firsts, d[l])
            olds = [adj_ref[b] for b in rows]
            for b, old, change in zip(rows, olds, sums):
                adj = old + change
                adj_ref[b] = adj
                put(1 - slot, b, (adj * sp_ref[l - 1, b]).astype(bf16).astype(f32), d[l - 1])

        over(lo, hi, d[l], backward)

    w0 = wb_ref[0]

    def last(firsts):
        rows, sums = convs(w0, 1, firsts, d[0])
        for b, change in zip(rows, sums):
            adj = adj_ref[b] + change
            hg_ref[pl.ds(b - HALO, 1), :] = jnp.sum(lift_w * adj, axis=0, keepdims=True)

    over(jnp.int32(HALO), jnp.int32(HALO + TR), d[0], last)

    hg = hg_ref[:TR, :TC]
    spans = {-1: (0, 8, 24), 0: (0, 24, 8), 1: (8, 32, 0), 2: (24, 32, 0)}
    message = []
    for block in ((0, 1), (2, -1)):
        lanes = jnp.zeros((1, TC), f32)
        for k in range(2):
            rows = []
            for p in range(NP):
                for dimple in block:
                    lo_r, hi_r, first = spans[dimple]
                    n = hi_r - lo_r
                    prod = hg[lo_r:hi_r] * s2_ref[k, 32 * p + first : 32 * p + first + n, :TC]
                    rows.append(jnp.sum(prod, axis=0, keepdims=True))
            rows += [jnp.zeros((4, TC), f32)]
            sums = jnp.concatenate(rows, axis=0)
            c = iota((TC, TC), 0)
            gather = jnp.where(((c + HALF) // SIDE - k + 1 == spot) & used, 1.0, 0.0)
            z = exact_dot(sums, gather.astype(bf16))
            lanes = lanes + jnp.sum(
                jnp.where(iota((16, TC), 0) == group, z, 0.0), axis=0, keepdims=True
            )
        message.append(lanes)

    def act_ext(dr):
        act = acts[dr, 0]
        act = act + jnp.where(spot == 0, pltpu.roll(acts[dr, -1], 120, 1), 0.0)
        return act + jnp.where(spot == 9, pltpu.roll(acts[dr, 1], 8, 1), 0.0)

    lane = iota((1, TC), 1)
    own_act = act_ext(0)
    ring_act = jnp.where(group % 2 == 0, act_ext(1), act_ext(-1))
    acc = jnp.sum(acc_ref[HALO : HALO + TR, :], axis=0, keepdims=True)
    local = 0.5 * jnp.sum(acc[:, :TC], axis=1, keepdims=True)
    first = jnp.where(used, message[0] * own_act, jnp.where(lane == 120, local, 0.0))
    ring = jnp.where(used, message[1] * ring_act, 0.0)
    whole_message = jnp.concatenate([first, ring], axis=1)
    out_ref[...] = jnp.broadcast_to(whole_message[None], out_ref.shape)


def final_kernel(grid, place_ref, design_ref, gathered2_ref, moved_ref, new_ref, obj_ref, whole_ref):
    row_count, col_count = grid
    whole, squares, misfit2 = combine(gathered2_ref[...].reshape(row_count * col_count, 2 * TC))
    lane = iota((1, 128), 1)
    whole_ref[...] = whole
    entries = float(row_count * col_count * NP * 16)
    cells = float(row_count * col_count * TR * TC)
    dev = place_ref[0] * col_count + place_ref[1]
    moved = moved_ref[...] + rate_of(squares, entries) * whole_ref[pl.ds(dev, 1), :]
    group, _, _ = lane_fields(128)
    by_group = jnp.where(iota((16, 128), 0) == group, moved, 0.0)
    lanes = iota((128, HALF), 0)
    pick = jnp.where((lanes % 10 == iota((128, HALF), 1) + 1) & (lanes < 120), 1.0, 0.0)
    change = exact_dot(by_group, pick.astype(bf16))
    for p in range(NP):
        new_ref[p] = design_ref[p] - change[2 * p : 2 * p + 2]
    misfit1 = jnp.sum(jnp.where(lane == 120, moved_ref[...], 0.0), axis=1, keepdims=True)
    obj_ref[0] = jnp.sum(misfit1) / cells
    obj_ref[1] = jnp.sum(misfit2) / cells


def vmem():
    return pl.BlockSpec(memory_space=pltpu.VMEM)


def smem():
    return pl.BlockSpec(memory_space=pltpu.SMEM)


def shape(dims, kind):
    return jax.ShapeDtypeStruct(dims, kind)


def params(mib):
    return pltpu.CompilerParams(vmem_limit_bytes=mib * MIB)


def on_device(
    row_count, col_count, design, active, stamp_basis, film_field, lift_weight, lift_bias,
    conv_weight, conv_bias, readout, target, dilation,
):
    grid = (row_count, col_count)
    place = jnp.stack([lax.axis_index("rows"), lax.axis_index("cols")]).astype(jnp.int32)
    one, two_up, two_down = pl.pallas_call(
        pack_kernel,
        out_shape=(shape((39, 16, TC), bf16), shape((34, 16, TC), bf16), shape((34, 16, TC), bf16)),
        in_specs=[vmem()] * 4,
        out_specs=(vmem(),) * 3,
        compiler_params=params(8),
        name="pack",
    )(film_field, design, active, target)

    def shifted(x, axis, by):
        count = lax.axis_size(axis)
        return lax.ppermute(x, axis, [(i, i + by) for i in range(count) if 0 <= i + by < count])

    u1, d1 = shifted(one, "rows", 1), shifted(one, "rows", -1)
    s2, expand = pl.pallas_call(
        prep_kernel,
        out_shape=(shape((2, NP * 32, WIDE), f32), shape((2, 384, WIDE), bf16)),
        in_specs=[vmem()],
        out_specs=(vmem(), vmem()),
        compiler_params=params(8),
        name="prep",
    )(stamp_basis.reshape(NP * 32, 32))
    u1, d1, s2, expand = lax.optimization_barrier((u1, d1, s2, expand))
    u2 = shifted(lax.dynamic_update_slice(two_up, u1[:1], (33, 0, 0)), "rows", 2)
    d2 = shifted(lax.dynamic_update_slice(two_down, d1[:1], (33, 0, 0)), "rows", -2)
    def paired(w):
        return jnp.concatenate(
            [jnp.pad(w, ((0, 0), (0, 0), (0, 48))), jnp.pad(w, ((0, 0), (0, 0), (48, 0)))], axis=1
        )

    wf = jnp.transpose(conv_weight, (0, 2, 1, 3)).reshape(LAYERS, 16, 144)
    wb = jnp.transpose(conv_weight[:, ::-1], (0, 3, 1, 2)).reshape(LAYERS, 16, 144)
    vec = jnp.concatenate(
        [lift_weight[None], lift_bias[None], readout[None], conv_bias], axis=0
    )[:, :, None]
    u2, d2, place = lax.optimization_barrier((u2, d2, place))
    tiles = (one, u1, u2, d1, d2)
    to_right, to_left = pl.pallas_call(
        halve_kernel,
        out_shape=(shape((SIDES, 16, TC), bf16),) * 2,
        in_specs=[vmem()] * 5,
        out_specs=(vmem(),) * 2,
        compiler_params=params(8),
        name="halve",
    )(*tiles)
    from_left = shifted(to_right, "cols", 1)
    from_right = shifted(to_left, "cols", -1)
    scratch = [
        pltpu.VMEM((SPARE + 1, 48, WIDE), bf16),
        pltpu.VMEM((SPARE + 1, 48, WIDE), bf16),
        pltpu.VMEM((LAYERS - 1, ROWS, 16, WIDE), f32),
        pltpu.VMEM((ROWS, 16, WIDE), f32),
        pltpu.VMEM((ROWS, WIDE), f32),
        pltpu.VMEM((TR + HALF, WIDE), f32),
        pltpu.VMEM((2, 112, WIDE), f32),
        pltpu.VMEM((ROWS, WIDE), f32),
    ]
    common = (place, dilation, vec, paired(wf), paired(wb), s2, expand, *tiles, from_left, from_right)
    specs = [smem(), smem()] + [vmem()] * 12

    def gather(message):
        return lax.all_to_all(message, ("rows", "cols"), 0, 0)

    devices = row_count * col_count
    message_shape = shape((devices, 1, 2 * TC), f32)

    message1 = pl.pallas_call(
        functools.partial(step_kernel, False, grid),
        out_shape=message_shape,
        in_specs=specs,
        out_specs=vmem(),
        scratch_shapes=scratch,
        compiler_params=params(30),
        name="step_one",
    )(*common)
    gathered1 = gather(message1)
    message2, moved = pl.pallas_call(
        functools.partial(step_kernel, True, grid),
        out_shape=(message_shape, shape((1, TC), f32)),
        in_specs=specs + [vmem()],
        out_specs=(vmem(), vmem()),
        scratch_shapes=[pltpu.VMEM((devices, TC), f32)] + scratch,
        compiler_params=params(30),
        name="step_two",
    )(*common, gathered1)
    gathered2 = gather(message2)
    new_design, objective = pl.pallas_call(
        functools.partial(final_kernel, grid),
        out_shape=(shape((NP, 2, HALF), f32), shape((2,), f32)),
        in_specs=[smem()] + [vmem()] * 3,
        out_specs=(vmem(), smem()),
        scratch_shapes=[pltpu.VMEM((devices, TC), f32)],
        compiler_params=params(8),
        name="finish",
    )(place, design, gathered2, moved)
    return new_design, objective


def solution(mesh):
    placed = (
        P(None, "rows", "cols"),
        P("rows", "cols"),
        P(),
        P(None, "rows", "cols"),
        P(),
        P(),
        P(),
        P(),
        P(),
        P("rows", "cols"),
        P(),
    )
    return jax.shard_map(
        functools.partial(on_device, mesh.shape["rows"], mesh.shape["cols"]),
        mesh=mesh,
        in_specs=placed,
        out_specs=(P(None, "rows", "cols"), P()),
        check_vma=False,
    )
```

```python
import functools

import jax
import jax.numpy as jnp
import numpy as np
from jax import lax
from jax.experimental import pallas as pl
from jax.experimental.pallas import tpu as pltpu
from jax.sharding import PartitionSpec as P

f32 = jnp.float32
bf16 = jnp.bfloat16
step_rate = 0.25
norm_eps = 1e-06

NP = 6
LAYERS = 4
SIDE = 16
HALF = 8
TR = 32
TC = 128
HALO = 64
WIDE = TC + 2 * HALO
ROWS = TR + 2 * HALO
SPARE = ROWS + 16
PAIRS = 16
MIB = 1024 * 1024


def iota(shape, dim):
    return lax.broadcasted_iota(jnp.int32, shape, dim)


def cell_col(dims):
    lane = iota(dims, 1)
    return jnp.where(lane < TC + HALO, lane, lane - WIDE)


def split3(x):
    hi = x.astype(bf16)
    rest = x - hi.astype(f32)
    mid = rest.astype(bf16)
    low = (rest - mid.astype(f32)).astype(bf16)
    return hi, mid, low


def dot(a, b):
    return jnp.dot(a, b, preferred_element_type=f32)


def exact_dot(x, ones):
    hi, mid, low = split3(x)
    return dot(hi, ones) + dot(mid, ones) + dot(low, ones)


def lane_fields(width):
    lane = iota((1, width), 1) % 128
    group = lane // 10
    return group, lane - 10 * group, lane < 120


def pack_kernel(
    film_hbm, design_hbm, active_hbm, target_hbm, one_ref, up_ref, down_ref,
    film_ref, design_ref, active_ref, target_ref, sems,
):
    reads = [
        pltpu.make_async_copy(src, dst, sems.at[n])
        for n, (src, dst) in enumerate(
            (
                (design_hbm, design_ref),
                (active_hbm, active_ref),
                (target_hbm, target_ref),
                (film_hbm, film_ref),
            )
        )
    ]
    for read in reads:
        read.start()
    for read in reads:
        read.wait()
    group, spot, used = lane_fields(TC)
    spread = jnp.where(
        (iota((HALF, TC), 0) == spot - 1) & used, 1.0, 0.0
    ).astype(bf16)
    active = active_ref[...].astype(f32)
    row_of = iota((2, TC), 0)
    amp_row = jnp.zeros((1, TC), f32)
    act_row = jnp.zeros((1, TC), f32)
    act_spread = exact_dot(active, spread)
    for p in range(NP):
        mine = row_of + 2 * p == group
        placed = jnp.where(mine, exact_dot(design_ref[p] * active, spread), 0.0)
        amp_row = amp_row + jnp.sum(placed, axis=0, keepdims=True)
        act_row = act_row + jnp.sum(jnp.where(mine, act_spread, 0.0), axis=0, keepdims=True)
    hi, mid, low = split3(amp_row)
    sub = iota((16, TC), 0)
    tile = jnp.where(sub == 0, hi.astype(f32), 0.0)
    tile = jnp.where(sub == 1, mid.astype(f32), tile)
    tile = jnp.where(sub == 2, low.astype(f32), tile)
    tile = jnp.where(sub == 3, act_row, tile).astype(bf16)
    one_ref[0] = tile
    up_ref[0] = tile
    down_ref[0] = tile
    film = jnp.swapaxes(film_ref[...].astype(f32), 0, 1).astype(bf16)
    one_ref[1 : 1 + TR] = film
    up_ref[1 : 1 + TR] = film
    down_ref[1 : 1 + TR] = film
    for n, piece in enumerate(split3(target_ref[...])):
        one_ref[33 + 2 * n] = piece[:16]
        one_ref[34 + 2 * n] = piece[16:]


SIDES = 96
AMPS = 89


def tile_pairs(u2, u1, own, d1, d2):
    pairs = [((u2, 1 + r), (u1, 1 + r)) for r in range(TR)]
    pairs += [((own, 1 + r), (own, 17 + r)) for r in range(16)]
    pairs += [((d1, 1 + r), (d2, 1 + r)) for r in range(TR)]
    pairs += [((u1, 33 + r), (d1, 33 + r)) for r in range(6)]
    return pairs + [((own, 33 + r), (own, 36 + r)) for r in range(3)]


def amp_tiles(u2, u1, own, d1, d2):
    return ((u2, 33), (u2, 0), (u1, 0), (own, 0), (d1, 0), (d2, 0), (d2, 33))


def swap_halves(x):
    return pltpu.roll(x, TC // 2, 1)


def halve_kernel(own_ref, u1_ref, u2_ref, d1_ref, d2_ref, right_ref, left_ref):
    low_half = iota((16, TC), 1) < HALO
    pairs = tile_pairs(u2_ref, u1_ref, own_ref, d1_ref, d2_ref)
    for n, ((ref_a, a), (ref_b, b)) in enumerate(pairs):
        first, second = ref_a[a].astype(f32), ref_b[b].astype(f32)
        right_ref[n] = jnp.where(low_half, swap_halves(first), second).astype(bf16)
        left_ref[n] = jnp.where(low_half, first, swap_halves(second)).astype(bf16)
    for n, (ref, at) in enumerate(amp_tiles(u2_ref, u1_ref, own_ref, d1_ref, d2_ref)):
        right_ref[AMPS + n] = ref[at]
        left_ref[AMPS + n] = ref[at]


def combine(gathered):
    own, ring = gathered[:, :128], gathered[:, 128:]
    group, spot, used = lane_fields(128)
    top = (group % 2 == 0) & used
    bottom = (group % 2 == 1) & used
    zero = jnp.zeros((16, 128), f32)
    above = jnp.concatenate([zero, ring[:240]], axis=0)
    below = jnp.concatenate([ring[16:], zero], axis=0)
    summed = own + jnp.where(top, above, 0.0) + jnp.where(bottom, below, 0.0)
    place = iota((256, 128), 0) % 16
    left = jnp.where(place == 0, 0.0, pltpu.roll(summed, 1, 0))
    right = jnp.where(place == 15, 0.0, pltpu.roll(summed, 255, 0))
    left = pltpu.roll(left, 120, 1)
    right = pltpu.roll(right, 8, 1)
    whole = summed + jnp.where(spot == 1, left, 0.0) + jnp.where(spot == 8, right, 0.0)
    whole = jnp.where((spot >= 1) & (spot <= 8) & used, whole, 0.0)
    squares = jnp.sum(jnp.sum(whole * whole, axis=0, keepdims=True), axis=1, keepdims=True)
    lane = iota((1, 128), 1)
    misfits = jnp.sum(
        jnp.where(lane == 120, jnp.sum(own, axis=0, keepdims=True), 0.0), axis=1, keepdims=True
    )
    return whole, squares, misfits


def rate_of(squares, entries):
    return step_rate / jnp.sqrt(squares / entries + norm_eps)


def prep_kernel(stamp_ref, s2_ref, expand_ref):
    for k in range(2):
        pick = jnp.where(
            iota((32, WIDE), 0) == (iota((32, WIDE), 1) + HALF) % SIDE + SIDE * k, 1.0, 0.0
        ).astype(bf16)
        s2_ref[k] = exact_dot(stamp_ref[...], pick)
    lane3 = iota((384, WIDE), 0)
    lane1 = lane3 % 128
    spot3 = lane1 % 10
    for k in range(2):
        b = (cell_col((384, WIDE)) + HALO + HALF) // SIDE - HALO // SIDE - k
        hit = (b == HALF * (lane3 // 128 - 1) + spot3 - 1) & (spot3 >= 1) & (spot3 <= 8)
        expand_ref[k] = jnp.where(hit & (lane1 < 120), 1.0, 0.0).astype(bf16)


def step_kernel(second, grid, *refs):
    row_count, col_count = grid
    (place_ref, vec_ref, wf_ref, wb_ref, s2_ref, expand_ref, own_ref, u1_ref, u2_ref, d1_ref,
     d2_ref, from_left_ref, from_right_ref) = refs[:13]
    rest = refs[13:]
    if second:
        gathered_ref, out_ref, moved_ref, whole_ref = rest[:4]
        rest = rest[4:]
    else:
        out_ref, rest = rest[0], rest[1:]
    cat0_ref, cat1_ref, sp_ref, adj_ref, height_ref, hg_ref, ampx_ref, acc_ref = rest
    my_row = place_ref[0]
    my_col = place_ref[1]
    group, spot, used = lane_fields(128)
    amps = amp_tiles(u2_ref, u1_ref, own_ref, d1_ref, d2_ref)

    if second:
        whole, squares, misfits = combine(gathered_ref[...].reshape(row_count * col_count, 2 * TC))
        whole_ref[...] = whole
        rate = rate_of(squares, float(row_count * col_count * NP * 16))
    masks = iota((16, 384), 0) == jnp.concatenate([group] * 3, axis=1)
    acts = {}
    stacked = []
    for dr in range(-3, 4):
        ref, at = amps[dr + 3]
        tiles = [from_left_ref[AMPS + dr + 3], ref[at], from_right_ref[AMPS + dr + 3]]
        pieces = []
        for dc, tile in zip((-1, 0, 1), tiles):
            t = tile.astype(f32)
            r, c = my_row + dr, my_col + dc
            inside = (r >= 0) & (r < row_count) & (c >= 0) & (c < col_count)
            t = t * jnp.where(inside, 1.0, 0.0)
            amp = t[0:1] + t[1:2] + t[2:3]
            if second:
                dev = jnp.where(inside, r * col_count + c, 0)
                moved = rate * whole_ref[pl.ds(dev, 1), :]
                moved = moved * jnp.where(inside, 1.0, 0.0)
                if dr == 0 and dc == 0:
                    moved_ref[...] = jnp.where(iota((1, TC), 1) == 120, misfits, moved)
                amp = amp - moved
            pieces.append(amp)
            acts[dr, dc] = t[3:4]
        row = jnp.concatenate(pieces, axis=1)
        stacked.append(jnp.where(masks, row, 0.0))
    stacked = jnp.concatenate(stacked, axis=0)
    for k in range(2):
        ampx_ref[k] = exact_dot(stacked, expand_ref[k])

    blocks = range(-4, 6)
    for half in range(2):
        totals = [jnp.zeros((HALF, WIDE), f32) for _ in blocks]
        for step, first in ((0, 16 * half if half else 8), (1 if half else -1, 0 if half else 24)):
            for p in range(NP):
                for k in range(2):
                    stamp = s2_ref[k, 32 * p + first : 32 * p + first + HALF, :]
                    for n, a in enumerate(blocks):
                        dr, i = (a + step) // 2, (a + step) % 2
                        row = 16 * (dr + 3) + 2 * p + i
                        totals[n] = totals[n] + stamp * ampx_ref[k, row : row + 1, :]
        for n, a in enumerate(blocks):
            start = HALO + SIDE * a + HALF * half
            height_ref[start : start + HALF, :] = totals[n]

    col = my_col * TC + cell_col((16, WIDE))
    in_map = (col >= 0) & (col < col_count * TC)

    cats = (cat0_ref, cat1_ref)

    def put(slot, b, value, shift):
        cat = cats[slot]
        b = jnp.where(b < map_hi, b, SPARE)
        value = jnp.where(in_map, value, 0.0)
        cat[b, 16:32, :] = value.astype(bf16)
        cat[b, 0:16, :] = pltpu.roll(value, shift, 1).astype(bf16)
        cat[b, 32:48, :] = pltpu.roll(value, WIDE - shift, 1).astype(bf16)

    def wide_row(ref):
        return jnp.broadcast_to(ref, (16, WIDE))

    lift_w = wide_row(vec_ref[0])
    map_lo = jnp.maximum(0, HALO - my_row * TR)
    map_hi = jnp.minimum(ROWS, HALO + (row_count - my_row) * TR)
    d = [place_ref[2 + l] for l in range(LAYERS)]
    total_d = d[0] + d[1] + d[2] + d[3]

    def bounds(reach):
        return jnp.maximum(map_lo, HALO - reach), jnp.minimum(map_hi, HALO + TR + reach)

    def over(lo, hi, dil, some_pairs):
        count = hi - lo
        whole = count // (2 * dil)
        pairs = whole * dil + jnp.minimum(dil, count - whole * 2 * dil)

        def some(number, base, i):
            firsts = []
            for _ in range(number):
                firsts.append(base + i)
                wrap = i + 1 >= dil
                next_base = jnp.where(wrap, base + 2 * dil, base)
                next_i = jnp.where(wrap, 0, i + 1)
                inside = next_base + next_i < hi
                base = jnp.where(inside, next_base, base)
                i = jnp.where(inside, next_i, i)
            some_pairs(firsts)
            return base, i

        full = pairs // PAIRS
        rest = pairs - PAIRS * full
        full = full + jnp.where(rest > PAIRS // 2, 1, 0)
        base, i = lax.fori_loop(
            0, full, lambda step, at: some(PAIRS, *at), (lo, jnp.int32(0))
        )

        @pl.when((rest > 0) & (rest <= PAIRS // 2))
        def _():
            some(PAIRS // 2, base, i)

    lo0, hi0 = bounds(2 * total_d)
    lift_b = wide_row(vec_ref[1])
    low_half = iota((16, TC), 1) < HALO

    def beside(place, second_row):
        left = from_left_ref[place].astype(f32)
        right = from_right_ref[place].astype(f32)
        if second_row:
            right = swap_halves(right)
        else:
            left = swap_halves(left)
        return jnp.where(low_half, right, left)

    spans = (
        (0, u2_ref, 0, TR, 0, False),
        (1, u1_ref, 0, TR, 0, True),
        (2, own_ref, 0, 16, 32, False),
        (2, own_ref, 16, 16, 32, True),
        (3, d1_ref, 0, TR, 48, False),
        (4, d2_ref, 0, TR, 48, True),
    )
    for n, ref, row0, count, place, second_row in spans:
        here = my_row + n - 2
        valid = (here >= 0) & (here < row_count)
        start = n * TR + row0
        first = jnp.clip(lo0 - start, 0, count)
        after = jnp.clip(hi0 - start, 0, count)

        def rows(step, _):
            r0 = jnp.minimum(first + step * 16, count - 16)
            hs = [height_ref[pl.ds(start + r0 + q, 1), :] for q in range(16)]
            for q in range(16):
                film = jnp.concatenate(
                    [
                        ref[1 + row0 + r0 + q].astype(f32),
                        beside(place + r0 + q, second_row),
                    ],
                    axis=1,
                )
                value = (lift_w * hs[q] + lift_b + film).astype(bf16).astype(f32)
                put(0, start + r0 + q, value, d[0])
            return 0

        lax.fori_loop(0, (after - first + 15) // 16, rows, 0)

        @pl.when(jnp.logical_not(valid))
        def _():
            def blank(r, _):
                cat0_ref[start + r] = jnp.zeros((48, WIDE), bf16)
                cat1_ref[start + r] = jnp.zeros((48, WIDE), bf16)
                return 0

            lax.fori_loop(0, count, blank, 0)

    def convs(w, slot, firsts, dil):
        cat = cats[slot]
        rows, sums = [], []
        for r in firsts:
            near = [cat[r - dil], cat[r], cat[r + dil], cat[r + 2 * dil]]
            both = dot(w, jnp.concatenate(near, axis=0))
            rows += [r, r + dil]
            sums += [both[:16], both[16:]]
        return rows, sums

    def parts(pre):
        s = 0.5 + 0.5 * jnp.tanh(0.5 * pre)
        silu = pre * s
        return silu, s + silu * (1.0 - s)

    reach = 2 * total_d
    for l in range(LAYERS - 1):
        slot = l % 2
        w = wf_ref[l]
        bias = wide_row(vec_ref[3 + l])
        reach = reach - d[l]
        lo, hi = bounds(reach)

        def forward(firsts):
            for b, pre in zip(*convs(w, slot, firsts, d[l])):
                silu, slope = parts(pre + bias)
                sp_ref[l, b] = slope
                value = cats[slot][b, 16:32, :].astype(f32) + silu
                put(1 - slot, b, value.astype(bf16).astype(f32), d[l + 1])

        over(lo, hi, d[l], forward)

    sides = (
        [(80 + r, False) for r in range(6)],
        [(86 + r % 3, r >= 3) for r in range(6)],
        [(80 + r, True) for r in range(6)],
    )
    for n, ref in enumerate((u1_ref, own_ref, d1_ref)):
        for half in range(2):
            target, side = jnp.zeros((16, TC), f32), jnp.zeros((16, TC), f32)
            for piece in (half, half + 2, half + 4):
                target = target + ref[33 + piece].astype(f32)
                side = side + beside(*sides[n][piece])
            first = TR * (n + 1) + 16 * half
            height_ref[first : first + 16, :TC] = target
            height_ref[first : first + 16, TC:] = side

    acc_ref[...] = jnp.zeros_like(acc_ref)
    lo, hi = bounds(total_d)
    w3 = wf_ref[3]
    bias3 = wide_row(vec_ref[6])
    readout = wide_row(vec_ref[2])

    def turn(firsts):
        rows, pres = convs(w3, 1, firsts, d[3])
        targets = [height_ref[pl.ds(b, 1), :] for b in rows]
        for b, pre, target in zip(rows, pres, targets):
            silu, slope = parts(pre + bias3)
            value = (cat1_ref[b, 16:32, :].astype(f32) + silu).astype(bf16).astype(f32)
            pressure = jnp.sum(readout * value, axis=0, keepdims=True)
            misfit = pressure - target
            acc_ref[pl.ds(b, 1), :] = misfit * misfit
            adj = readout * (misfit * (1.0 / (SIDE * SIDE)))
            adj_ref[b] = adj
            put(0, b, (adj * slope).astype(bf16).astype(f32), d[3])

    over(lo, hi, d[3], turn)

    reach = total_d
    for l in range(LAYERS - 1, 0, -1):
        slot = (l + 1) % 2
        wb = wb_ref[l]
        reach = reach - d[l]
        lo, hi = bounds(reach)

        def backward(firsts):
            rows, sums = convs(wb, slot, firsts, d[l])
            olds = [adj_ref[b] for b in rows]
            for b, old, change in zip(rows, olds, sums):
                adj = old + change
                adj_ref[b] = adj
                put(1 - slot, b, (adj * sp_ref[l - 1, b]).astype(bf16).astype(f32), d[l - 1])

        over(lo, hi, d[l], backward)

    w0 = wb_ref[0]

    def last(firsts):
        rows, sums = convs(w0, 1, firsts, d[0])
        for b, change in zip(rows, sums):
            adj = adj_ref[b] + change
            hg_ref[pl.ds(b - HALO, 1), :] = jnp.sum(lift_w * adj, axis=0, keepdims=True)

    over(jnp.int32(HALO), jnp.int32(HALO + TR), d[0], last)

    hg = hg_ref[:TR, :TC]
    spans = {-1: (0, 8, 24), 0: (0, 24, 8), 1: (8, 32, 0), 2: (24, 32, 0)}
    message = []
    for block in ((0, 1), (2, -1)):
        lanes = jnp.zeros((1, TC), f32)
        for k in range(2):
            rows = []
            for p in range(NP):
                for dimple in block:
                    lo_r, hi_r, first = spans[dimple]
                    n = hi_r - lo_r
                    prod = hg[lo_r:hi_r] * s2_ref[k, 32 * p + first : 32 * p + first + n, :TC]
                    rows.append(jnp.sum(prod, axis=0, keepdims=True))
            rows += [jnp.zeros((4, TC), f32)]
            sums = jnp.concatenate(rows, axis=0)
            c = iota((TC, TC), 0)
            gather = jnp.where(((c + HALF) // SIDE - k + 1 == spot) & used, 1.0, 0.0)
            z = exact_dot(sums, gather.astype(bf16))
            lanes = lanes + jnp.sum(
                jnp.where(iota((16, TC), 0) == group, z, 0.0), axis=0, keepdims=True
            )
        message.append(lanes)

    def act_ext(dr):
        act = acts[dr, 0]
        act = act + jnp.where(spot == 0, pltpu.roll(acts[dr, -1], 120, 1), 0.0)
        return act + jnp.where(spot == 9, pltpu.roll(acts[dr, 1], 8, 1), 0.0)

    lane = iota((1, TC), 1)
    own_act = act_ext(0)
    ring_act = jnp.where(group % 2 == 0, act_ext(1), act_ext(-1))
    acc = jnp.sum(acc_ref[HALO : HALO + TR, :], axis=0, keepdims=True)
    local = 0.5 * jnp.sum(acc[:, :TC], axis=1, keepdims=True)
    first = jnp.where(used, message[0] * own_act, jnp.where(lane == 120, local, 0.0))
    ring = jnp.where(used, message[1] * ring_act, 0.0)
    whole_message = jnp.concatenate([first, ring], axis=1)
    out_ref[...] = jnp.broadcast_to(whole_message[None], out_ref.shape)


def final_kernel(grid, place_ref, design_ref, gathered2_ref, moved_ref, new_ref, obj_ref, whole_ref):
    row_count, col_count = grid
    whole, squares, misfit2 = combine(gathered2_ref[...].reshape(row_count * col_count, 2 * TC))
    lane = iota((1, 128), 1)
    whole_ref[...] = whole
    entries = float(row_count * col_count * NP * 16)
    cells = float(row_count * col_count * TR * TC)
    dev = place_ref[0] * col_count + place_ref[1]
    moved = moved_ref[...] + rate_of(squares, entries) * whole_ref[pl.ds(dev, 1), :]
    group, _, _ = lane_fields(128)
    by_group = jnp.where(iota((16, 128), 0) == group, moved, 0.0)
    lanes = iota((128, HALF), 0)
    pick = jnp.where((lanes % 10 == iota((128, HALF), 1) + 1) & (lanes < 120), 1.0, 0.0)
    change = exact_dot(by_group, pick.astype(bf16))
    for p in range(NP):
        new_ref[p] = design_ref[p] - change[2 * p : 2 * p + 2]
    misfit1 = jnp.sum(jnp.where(lane == 120, moved_ref[...], 0.0), axis=1, keepdims=True)
    obj_ref[0] = jnp.sum(misfit1) / cells
    obj_ref[1] = jnp.sum(misfit2) / cells


def vmem():
    return pl.BlockSpec(memory_space=pltpu.VMEM)


def smem():
    return pl.BlockSpec(memory_space=pltpu.SMEM)


def shape(dims, kind):
    return jax.ShapeDtypeStruct(dims, kind)


def params(mib):
    return pltpu.CompilerParams(vmem_limit_bytes=mib * MIB)


def on_device(
    row_count, col_count, design, active, stamp_basis, film_field, lift_weight, lift_bias,
    conv_weight, conv_bias, readout, target, dilation,
):
    grid = (row_count, col_count)
    here = jnp.stack([lax.axis_index("rows"), lax.axis_index("cols")]).astype(jnp.int32)
    place = jnp.concatenate([here, dilation])
    one, two_up, two_down = pl.pallas_call(
        pack_kernel,
        out_shape=(shape((39, 16, TC), bf16), shape((34, 16, TC), bf16), shape((34, 16, TC), bf16)),
        in_specs=[pl.BlockSpec(memory_space=pltpu.HBM)] * 4,
        out_specs=(vmem(),) * 3,
        scratch_shapes=[
            pltpu.VMEM(film_field.shape, bf16),
            pltpu.VMEM(design.shape, f32),
            pltpu.VMEM(active.shape, jnp.int32),
            pltpu.VMEM(target.shape, f32),
            pltpu.SemaphoreType.DMA((4,)),
        ],
        compiler_params=params(8),
        name="pack",
    )(*[pltpu.with_memory_space_constraint(x, pltpu.HBM) for x in (film_field, design, active, target)])

    def shifted(x, axis, by):
        count = lax.axis_size(axis)
        return lax.ppermute(x, axis, [(i, (i + by) % count) for i in range(count)])

    u1, d1 = shifted(one, "rows", 1), shifted(one, "rows", -1)
    s2, expand = pl.pallas_call(
        prep_kernel,
        out_shape=(shape((2, NP * 32, WIDE), f32), shape((2, 384, WIDE), bf16)),
        in_specs=[vmem()],
        out_specs=(vmem(), vmem()),
        compiler_params=params(8),
        name="prep",
    )(stamp_basis.reshape(NP * 32, 32))
    u1, d1, s2, expand = lax.optimization_barrier((u1, d1, s2, expand))
    u2 = shifted(lax.dynamic_update_slice(two_up, u1[:1], (33, 0, 0)), "rows", 2)
    d2 = shifted(lax.dynamic_update_slice(two_down, d1[:1], (33, 0, 0)), "rows", -2)
    def paired(w):
        return jnp.concatenate(
            [jnp.pad(w, ((0, 0), (0, 0), (0, 48))), jnp.pad(w, ((0, 0), (0, 0), (48, 0)))], axis=1
        )

    wf = jnp.transpose(conv_weight, (0, 2, 1, 3)).reshape(LAYERS, 16, 144)
    wb = jnp.transpose(conv_weight[:, ::-1], (0, 3, 1, 2)).reshape(LAYERS, 16, 144)
    vec = jnp.concatenate(
        [lift_weight[None], lift_bias[None], readout[None], conv_bias], axis=0
    )[:, :, None]
    u2, d2, place = lax.optimization_barrier((u2, d2, place))
    tiles = (one, u1, u2, d1, d2)
    to_right, to_left = pl.pallas_call(
        halve_kernel,
        out_shape=(shape((SIDES, 16, TC), bf16),) * 2,
        in_specs=[vmem()] * 5,
        out_specs=(vmem(),) * 2,
        compiler_params=params(8),
        name="halve",
    )(*tiles)
    from_left = shifted(to_right, "cols", 1)
    from_right = shifted(to_left, "cols", -1)
    scratch = [
        pltpu.VMEM((SPARE + 1, 48, WIDE), bf16),
        pltpu.VMEM((SPARE + 1, 48, WIDE), bf16),
        pltpu.VMEM((LAYERS - 1, ROWS, 16, WIDE), f32),
        pltpu.VMEM((ROWS, 16, WIDE), f32),
        pltpu.VMEM((ROWS, WIDE), f32),
        pltpu.VMEM((TR + HALF, WIDE), f32),
        pltpu.VMEM((2, 112, WIDE), f32),
        pltpu.VMEM((ROWS, WIDE), f32),
    ]
    common = (place, vec, paired(wf), paired(wb), s2, expand, *tiles, from_left, from_right)
    specs = [smem()] + [vmem()] * 12

    def gather(message):
        return lax.all_to_all(message, ("rows", "cols"), 0, 0)

    devices = row_count * col_count
    message_shape = shape((devices, 1, 2 * TC), f32)

    message1 = pl.pallas_call(
        functools.partial(step_kernel, False, grid),
        out_shape=message_shape,
        in_specs=specs,
        out_specs=vmem(),
        scratch_shapes=scratch,
        compiler_params=params(30),
        name="step_one",
    )(*common)
    gathered1 = gather(message1)
    message2, moved = pl.pallas_call(
        functools.partial(step_kernel, True, grid),
        out_shape=(message_shape, shape((1, TC), f32)),
        in_specs=specs + [vmem()],
        out_specs=(vmem(), vmem()),
        scratch_shapes=[pltpu.VMEM((devices, TC), f32)] + scratch,
        compiler_params=params(30),
        name="step_two",
    )(*common, gathered1)
    gathered2 = gather(message2)
    new_design, objective = pl.pallas_call(
        functools.partial(final_kernel, grid),
        out_shape=(shape((NP, 2, HALF), f32), shape((2,), f32)),
        in_specs=[smem()] + [vmem()] * 3,
        out_specs=(vmem(), smem()),
        scratch_shapes=[pltpu.VMEM((devices, TC), f32)],
        compiler_params=params(8),
        name="finish",
    )(place, design, gathered2, moved)
    return new_design, objective


def solution(mesh):
    placed = (
        P(None, "rows", "cols"),
        P("rows", "cols"),
        P(),
        P(None, "rows", "cols"),
        P(),
        P(),
        P(),
        P(),
        P(),
        P("rows", "cols"),
        P(),
    )
    return jax.shard_map(
        functools.partial(on_device, mesh.shape["rows"], mesh.shape["cols"]),
        mesh=mesh,
        in_specs=placed,
        out_specs=(P(None, "rows", "cols"), P()),
        check_vma=False,
    )
```

```python
import functools

import jax
import jax.numpy as jnp
import numpy as np
from jax import lax
from jax.experimental import pallas as pl
from jax.experimental.pallas import tpu as pltpu
from jax.sharding import PartitionSpec as P

f32 = jnp.float32
bf16 = jnp.bfloat16
step_rate = 0.25
norm_eps = 1e-06

NP = 6
LAYERS = 4
SIDE = 16
HALF = 8
TR = 32
TC = 128
HALO = 64
WIDE = TC + 2 * HALO
ROWS = TR + 2 * HALO
SPARE = ROWS + 16
PAIRS = 16
MIB = 1024 * 1024


def iota(shape, dim):
    return lax.broadcasted_iota(jnp.int32, shape, dim)


def cell_col(dims):
    lane = iota(dims, 1)
    return jnp.where(lane < TC + HALO, lane, lane - WIDE)


def split3(x):
    hi = x.astype(bf16)
    rest = x - hi.astype(f32)
    mid = rest.astype(bf16)
    low = (rest - mid.astype(f32)).astype(bf16)
    return hi, mid, low


def dot(a, b):
    return jnp.dot(a, b, preferred_element_type=f32)


def exact_dot(x, ones):
    hi, mid, low = split3(x)
    return dot(hi, ones) + dot(mid, ones) + dot(low, ones)


def lane_fields(width):
    lane = iota((1, width), 1) % 128
    group = lane // 10
    return group, lane - 10 * group, lane < 120


def pack_kernel(
    film_hbm, design_hbm, active_hbm, target_hbm, one_ref, two_ref, three_ref,
    film_ref, design_ref, active_ref, target_ref, sems,
):
    reads = [
        pltpu.make_async_copy(src, dst, sems.at[n])
        for n, (src, dst) in enumerate(
            (
                (design_hbm, design_ref),
                (active_hbm, active_ref),
                (target_hbm, target_ref),
                (film_hbm, film_ref),
            )
        )
    ]
    for read in reads:
        read.start()
    for read in reads:
        read.wait()
    group, spot, used = lane_fields(TC)
    spread = jnp.where(
        (iota((HALF, TC), 0) == spot - 1) & used, 1.0, 0.0
    ).astype(bf16)
    active = active_ref[...].astype(f32)
    row_of = iota((2, TC), 0)
    amp_row = jnp.zeros((1, TC), f32)
    act_row = jnp.zeros((1, TC), f32)
    act_spread = exact_dot(active, spread)
    for p in range(NP):
        mine = row_of + 2 * p == group
        placed = jnp.where(mine, exact_dot(design_ref[p] * active, spread), 0.0)
        amp_row = amp_row + jnp.sum(placed, axis=0, keepdims=True)
        act_row = act_row + jnp.sum(jnp.where(mine, act_spread, 0.0), axis=0, keepdims=True)
    hi, mid, low = split3(amp_row)
    sub = iota((16, TC), 0)
    tile = jnp.where(sub == 0, hi.astype(f32), 0.0)
    tile = jnp.where(sub == 1, mid.astype(f32), tile)
    tile = jnp.where(sub == 2, low.astype(f32), tile)
    tile = jnp.where(sub == 3, act_row, tile).astype(bf16)
    one_ref[0] = tile
    two_ref[0] = tile
    three_ref[0] = tile
    film = jnp.swapaxes(film_ref[...].astype(f32), 0, 1).astype(bf16)
    one_ref[1 : 1 + TR] = film
    two_ref[1 : 1 + TR] = film
    for n, piece in enumerate(split3(target_ref[...])):
        one_ref[33 + 2 * n] = piece[:16]
        one_ref[34 + 2 * n] = piece[16:]


SIDES = 96
AMPS = 89


def tile_pairs(u2, u1, own, d1, d2):
    pairs = [((u2, 1 + r), (u1, 1 + r)) for r in range(TR)]
    pairs += [((own, 1 + r), (own, 17 + r)) for r in range(16)]
    pairs += [((d1, 1 + r), (d2, 1 + r)) for r in range(TR)]
    pairs += [((u1, 33 + r), (d1, 33 + r)) for r in range(6)]
    return pairs + [((own, 33 + r), (own, 36 + r)) for r in range(3)]


def amp_tiles(u2, u1, own, d1, d2, far):
    return (far, 0), (u2, 0), (u1, 0), (own, 0), (d1, 0), (d2, 0), (far, 1)


def swap_halves(x):
    return pltpu.roll(x, TC // 2, 1)


def halve_kernel(
    own_ref, u1_ref, u2_ref, d1_ref, d2_ref, far_ref, right_ref, left_ref
):
    low_half = iota((16, TC), 1) < HALO
    pairs = tile_pairs(u2_ref, u1_ref, own_ref, d1_ref, d2_ref)
    for n, ((ref_a, a), (ref_b, b)) in enumerate(pairs):
        first, second = ref_a[a].astype(f32), ref_b[b].astype(f32)
        right_ref[n] = jnp.where(low_half, swap_halves(first), second).astype(bf16)
        left_ref[n] = jnp.where(low_half, first, swap_halves(second)).astype(bf16)
    amps = amp_tiles(u2_ref, u1_ref, own_ref, d1_ref, d2_ref, far_ref)
    for n, (ref, at) in enumerate(amps):
        right_ref[AMPS + n] = ref[at]
        left_ref[AMPS + n] = ref[at]


def combine(gathered):
    own, ring = gathered[:, :128], gathered[:, 128:]
    group, spot, used = lane_fields(128)
    top = (group % 2 == 0) & used
    bottom = (group % 2 == 1) & used
    zero = jnp.zeros((16, 128), f32)
    above = jnp.concatenate([zero, ring[:240]], axis=0)
    below = jnp.concatenate([ring[16:], zero], axis=0)
    summed = own + jnp.where(top, above, 0.0) + jnp.where(bottom, below, 0.0)
    place = iota((256, 128), 0) % 16
    left = jnp.where(place == 0, 0.0, pltpu.roll(summed, 1, 0))
    right = jnp.where(place == 15, 0.0, pltpu.roll(summed, 255, 0))
    left = pltpu.roll(left, 120, 1)
    right = pltpu.roll(right, 8, 1)
    whole = summed + jnp.where(spot == 1, left, 0.0) + jnp.where(spot == 8, right, 0.0)
    whole = jnp.where((spot >= 1) & (spot <= 8) & used, whole, 0.0)
    squares = jnp.sum(jnp.sum(whole * whole, axis=0, keepdims=True), axis=1, keepdims=True)
    lane = iota((1, 128), 1)
    misfits = jnp.sum(
        jnp.where(lane == 120, jnp.sum(own, axis=0, keepdims=True), 0.0), axis=1, keepdims=True
    )
    return whole, squares, misfits


def rate_of(squares, entries):
    return step_rate / jnp.sqrt(squares / entries + norm_eps)


def prep_kernel(stamp_ref, s2_ref, expand_ref):
    for k in range(2):
        pick = jnp.where(
            iota((32, WIDE), 0) == (iota((32, WIDE), 1) + HALF) % SIDE + SIDE * k, 1.0, 0.0
        ).astype(bf16)
        s2_ref[k] = exact_dot(stamp_ref[...], pick)
    lane3 = iota((384, WIDE), 0)
    lane1 = lane3 % 128
    spot3 = lane1 % 10
    for k in range(2):
        b = (cell_col((384, WIDE)) + HALO + HALF) // SIDE - HALO // SIDE - k
        hit = (b == HALF * (lane3 // 128 - 1) + spot3 - 1) & (spot3 >= 1) & (spot3 <= 8)
        expand_ref[k] = jnp.where(hit & (lane1 < 120), 1.0, 0.0).astype(bf16)


def step_kernel(second, grid, *refs):
    row_count, col_count = grid
    (place_ref, vec_ref, wf_ref, wb_ref, s2_ref, expand_ref, own_ref, u1_ref, u2_ref,
     d1_ref, d2_ref, far_ref, from_left_ref, from_right_ref) = refs[:14]
    rest = refs[14:]
    if second:
        gathered_ref, out_ref, moved_ref, whole_ref = rest[:4]
        rest = rest[4:]
    else:
        out_ref, rest = rest[0], rest[1:]
    cat0_ref, cat1_ref, sp_ref, adj_ref, height_ref, hg_ref, ampx_ref, acc_ref = rest
    my_row = place_ref[0]
    my_col = place_ref[1]
    group, spot, used = lane_fields(128)
    amps = amp_tiles(u2_ref, u1_ref, own_ref, d1_ref, d2_ref, far_ref)

    if second:
        whole, squares, misfits = combine(gathered_ref[...].reshape(row_count * col_count, 2 * TC))
        whole_ref[...] = whole
        rate = rate_of(squares, float(row_count * col_count * NP * 16))
    masks = iota((16, 384), 0) == jnp.concatenate([group] * 3, axis=1)
    acts = {}
    stacked = []
    for dr in range(-3, 4):
        ref, at = amps[dr + 3]
        tiles = [from_left_ref[AMPS + dr + 3], ref[at], from_right_ref[AMPS + dr + 3]]
        pieces = []
        for dc, tile in zip((-1, 0, 1), tiles):
            t = tile.astype(f32)
            r, c = my_row + dr, my_col + dc
            inside = (r >= 0) & (r < row_count) & (c >= 0) & (c < col_count)
            t = t * jnp.where(inside, 1.0, 0.0)
            amp = t[0:1] + t[1:2] + t[2:3]
            if second:
                dev = jnp.where(inside, r * col_count + c, 0)
                moved = rate * whole_ref[pl.ds(dev, 1), :]
                moved = moved * jnp.where(inside, 1.0, 0.0)
                if dr == 0 and dc == 0:
                    moved_ref[...] = jnp.where(iota((1, TC), 1) == 120, misfits, moved)
                amp = amp - moved
            pieces.append(amp)
            acts[dr, dc] = t[3:4]
        row = jnp.concatenate(pieces, axis=1)
        stacked.append(jnp.where(masks, row, 0.0))
    stacked = jnp.concatenate(stacked, axis=0)
    for k in range(2):
        ampx_ref[k] = exact_dot(stacked, expand_ref[k])

    blocks = range(-4, 6)
    for half in range(2):
        totals = [jnp.zeros((HALF, WIDE), f32) for _ in blocks]
        for step, first in ((0, 16 * half if half else 8), (1 if half else -1, 0 if half else 24)):
            for p in range(NP):
                for k in range(2):
                    stamp = s2_ref[k, 32 * p + first : 32 * p + first + HALF, :]
                    for n, a in enumerate(blocks):
                        dr, i = (a + step) // 2, (a + step) % 2
                        row = 16 * (dr + 3) + 2 * p + i
                        totals[n] = totals[n] + stamp * ampx_ref[k, row : row + 1, :]
        for n, a in enumerate(blocks):
            start = HALO + SIDE * a + HALF * half
            height_ref[start : start + HALF, :] = totals[n]

    col = my_col * TC + cell_col((16, WIDE))
    in_map = (col >= 0) & (col < col_count * TC)

    cats = (cat0_ref, cat1_ref)

    def put(slot, b, value, shift):
        cat = cats[slot]
        b = jnp.where(b < map_hi, b, SPARE)
        value = jnp.where(in_map, value, 0.0)
        cat[b, 16:32, :] = value.astype(bf16)
        cat[b, 0:16, :] = pltpu.roll(value, shift, 1).astype(bf16)
        cat[b, 32:48, :] = pltpu.roll(value, WIDE - shift, 1).astype(bf16)

    def wide_row(ref):
        return jnp.broadcast_to(ref, (16, WIDE))

    lift_w = wide_row(vec_ref[0])
    map_lo = jnp.maximum(0, HALO - my_row * TR)
    map_hi = jnp.minimum(ROWS, HALO + (row_count - my_row) * TR)
    d = [place_ref[2 + l] for l in range(LAYERS)]
    total_d = d[0] + d[1] + d[2] + d[3]

    def bounds(reach):
        return jnp.maximum(map_lo, HALO - reach), jnp.minimum(map_hi, HALO + TR + reach)

    def over(lo, hi, dil, some_pairs):
        count = hi - lo
        whole = count // (2 * dil)
        pairs = whole * dil + jnp.minimum(dil, count - whole * 2 * dil)

        def some(number, base, i):
            firsts = []
            for _ in range(number):
                firsts.append(base + i)
                wrap = i + 1 >= dil
                next_base = jnp.where(wrap, base + 2 * dil, base)
                next_i = jnp.where(wrap, 0, i + 1)
                inside = next_base + next_i < hi
                base = jnp.where(inside, next_base, base)
                i = jnp.where(inside, next_i, i)
            some_pairs(firsts)
            return base, i

        full = pairs // PAIRS
        rest = pairs - PAIRS * full
        full = full + jnp.where(rest > PAIRS // 2, 1, 0)
        base, i = lax.fori_loop(
            0, full, lambda step, at: some(PAIRS, *at), (lo, jnp.int32(0))
        )

        @pl.when((rest > 0) & (rest <= PAIRS // 2))
        def _():
            some(PAIRS // 2, base, i)

    lo0, hi0 = bounds(2 * total_d)
    lift_b = wide_row(vec_ref[1])
    low_half = iota((16, TC), 1) < HALO

    def beside(place, second_row):
        left = from_left_ref[place].astype(f32)
        right = from_right_ref[place].astype(f32)
        if second_row:
            right = swap_halves(right)
        else:
            left = swap_halves(left)
        return jnp.where(low_half, right, left)

    spans = (
        (0, u2_ref, 0, TR, 0, False),
        (1, u1_ref, 0, TR, 0, True),
        (2, own_ref, 0, 16, 32, False),
        (2, own_ref, 16, 16, 32, True),
        (3, d1_ref, 0, TR, 48, False),
        (4, d2_ref, 0, TR, 48, True),
    )
    for n, ref, row0, count, place, second_row in spans:
        here = my_row + n - 2
        valid = (here >= 0) & (here < row_count)
        start = n * TR + row0
        first = jnp.clip(lo0 - start, 0, count)
        after = jnp.clip(hi0 - start, 0, count)

        def rows(step, _):
            r0 = jnp.minimum(first + step * 16, count - 16)
            hs = [height_ref[pl.ds(start + r0 + q, 1), :] for q in range(16)]
            for q in range(16):
                film = jnp.concatenate(
                    [
                        ref[1 + row0 + r0 + q].astype(f32),
                        beside(place + r0 + q, second_row),
                    ],
                    axis=1,
                )
                value = (lift_w * hs[q] + lift_b + film).astype(bf16).astype(f32)
                put(0, start + r0 + q, value, d[0])
            return 0

        lax.fori_loop(0, (after - first + 15) // 16, rows, 0)

        @pl.when(jnp.logical_not(valid))
        def _():
            def blank(r, _):
                cat0_ref[start + r] = jnp.zeros((48, WIDE), bf16)
                cat1_ref[start + r] = jnp.zeros((48, WIDE), bf16)
                return 0

            lax.fori_loop(0, count, blank, 0)

    def convs(w, slot, firsts, dil):
        cat = cats[slot]
        rows, sums = [], []
        for r in firsts:
            near = [cat[r - dil], cat[r], cat[r + dil], cat[r + 2 * dil]]
            both = dot(w, jnp.concatenate(near, axis=0))
            rows += [r, r + dil]
            sums += [both[:16], both[16:]]
        return rows, sums

    def parts(pre):
        s = 0.5 + 0.5 * jnp.tanh(0.5 * pre)
        silu = pre * s
        return silu, s + silu * (1.0 - s)

    reach = 2 * total_d
    for l in range(LAYERS - 1):
        slot = l % 2
        w = wf_ref[l]
        bias = wide_row(vec_ref[3 + l])
        reach = reach - d[l]
        lo, hi = bounds(reach)

        def forward(firsts):
            for b, pre in zip(*convs(w, slot, firsts, d[l])):
                silu, slope = parts(pre + bias)
                sp_ref[l, b] = slope
                value = cats[slot][b, 16:32, :].astype(f32) + silu
                put(1 - slot, b, value.astype(bf16).astype(f32), d[l + 1])

        over(lo, hi, d[l], forward)

    sides = (
        [(80 + r, False) for r in range(6)],
        [(86 + r % 3, r >= 3) for r in range(6)],
        [(80 + r, True) for r in range(6)],
    )
    for n, ref in enumerate((u1_ref, own_ref, d1_ref)):
        for half in range(2):
            target, side = jnp.zeros((16, TC), f32), jnp.zeros((16, TC), f32)
            for piece in (half, half + 2, half + 4):
                target = target + ref[33 + piece].astype(f32)
                side = side + beside(*sides[n][piece])
            first = TR * (n + 1) + 16 * half
            height_ref[first : first + 16, :TC] = target
            height_ref[first : first + 16, TC:] = side

    acc_ref[...] = jnp.zeros_like(acc_ref)
    lo, hi = bounds(total_d)
    w3 = wf_ref[3]
    bias3 = wide_row(vec_ref[6])
    readout = wide_row(vec_ref[2])

    def turn(firsts):
        rows, pres = convs(w3, 1, firsts, d[3])
        targets = [height_ref[pl.ds(b, 1), :] for b in rows]
        for b, pre, target in zip(rows, pres, targets):
            silu, slope = parts(pre + bias3)
            value = (cat1_ref[b, 16:32, :].astype(f32) + silu).astype(bf16).astype(f32)
            pressure = jnp.sum(readout * value, axis=0, keepdims=True)
            misfit = pressure - target
            acc_ref[pl.ds(b, 1), :] = misfit * misfit
            adj = readout * (misfit * (1.0 / (SIDE * SIDE)))
            adj_ref[b] = adj
            put(0, b, (adj * slope).astype(bf16).astype(f32), d[3])

    over(lo, hi, d[3], turn)

    reach = total_d
    for l in range(LAYERS - 1, 0, -1):
        slot = (l + 1) % 2
        wb = wb_ref[l]
        reach = reach - d[l]
        lo, hi = bounds(reach)

        def backward(firsts):
            rows, sums = convs(wb, slot, firsts, d[l])
            olds = [adj_ref[b] for b in rows]
            for b, old, change in zip(rows, olds, sums):
                adj = old + change
                adj_ref[b] = adj
                put(1 - slot, b, (adj * sp_ref[l - 1, b]).astype(bf16).astype(f32), d[l - 1])

        over(lo, hi, d[l], backward)

    w0 = wb_ref[0]

    def last(firsts):
        rows, sums = convs(w0, 1, firsts, d[0])
        for b, change in zip(rows, sums):
            adj = adj_ref[b] + change
            hg_ref[pl.ds(b - HALO, 1), :] = jnp.sum(lift_w * adj, axis=0, keepdims=True)

    over(jnp.int32(HALO), jnp.int32(HALO + TR), d[0], last)

    hg = hg_ref[:TR, :TC]
    spans = {-1: (0, 8, 24), 0: (0, 24, 8), 1: (8, 32, 0), 2: (24, 32, 0)}
    message = []
    for block in ((0, 1), (2, -1)):
        lanes = jnp.zeros((1, TC), f32)
        for k in range(2):
            rows = []
            for p in range(NP):
                for dimple in block:
                    lo_r, hi_r, first = spans[dimple]
                    n = hi_r - lo_r
                    prod = hg[lo_r:hi_r] * s2_ref[k, 32 * p + first : 32 * p + first + n, :TC]
                    rows.append(jnp.sum(prod, axis=0, keepdims=True))
            rows += [jnp.zeros((4, TC), f32)]
            sums = jnp.concatenate(rows, axis=0)
            c = iota((TC, TC), 0)
            gather = jnp.where(((c + HALF) // SIDE - k + 1 == spot) & used, 1.0, 0.0)
            z = exact_dot(sums, gather.astype(bf16))
            lanes = lanes + jnp.sum(
                jnp.where(iota((16, TC), 0) == group, z, 0.0), axis=0, keepdims=True
            )
        message.append(lanes)

    def act_ext(dr):
        act = acts[dr, 0]
        act = act + jnp.where(spot == 0, pltpu.roll(acts[dr, -1], 120, 1), 0.0)
        return act + jnp.where(spot == 9, pltpu.roll(acts[dr, 1], 8, 1), 0.0)

    lane = iota((1, TC), 1)
    own_act = act_ext(0)
    ring_act = jnp.where(group % 2 == 0, act_ext(1), act_ext(-1))
    acc = jnp.sum(acc_ref[HALO : HALO + TR, :], axis=0, keepdims=True)
    local = 0.5 * jnp.sum(acc[:, :TC], axis=1, keepdims=True)
    first = jnp.where(used, message[0] * own_act, jnp.where(lane == 120, local, 0.0))
    ring = jnp.where(used, message[1] * ring_act, 0.0)
    whole_message = jnp.concatenate([first, ring], axis=1)
    out_ref[...] = jnp.broadcast_to(whole_message[None], out_ref.shape)


def final_kernel(grid, place_ref, design_ref, gathered2_ref, moved_ref, new_ref, obj_ref, whole_ref):
    row_count, col_count = grid
    whole, squares, misfit2 = combine(gathered2_ref[...].reshape(row_count * col_count, 2 * TC))
    lane = iota((1, 128), 1)
    whole_ref[...] = whole
    entries = float(row_count * col_count * NP * 16)
    cells = float(row_count * col_count * TR * TC)
    dev = place_ref[0] * col_count + place_ref[1]
    moved = moved_ref[...] + rate_of(squares, entries) * whole_ref[pl.ds(dev, 1), :]
    group, _, _ = lane_fields(128)
    by_group = jnp.where(iota((16, 128), 0) == group, moved, 0.0)
    lanes = iota((128, HALF), 0)
    pick = jnp.where((lanes % 10 == iota((128, HALF), 1) + 1) & (lanes < 120), 1.0, 0.0)
    change = exact_dot(by_group, pick.astype(bf16))
    for p in range(NP):
        new_ref[p] = design_ref[p] - change[2 * p : 2 * p + 2]
    misfit1 = jnp.sum(jnp.where(lane == 120, moved_ref[...], 0.0), axis=1, keepdims=True)
    obj_ref[0] = jnp.sum(misfit1) / cells
    obj_ref[1] = jnp.sum(misfit2) / cells


def vmem():
    return pl.BlockSpec(memory_space=pltpu.VMEM)


def smem():
    return pl.BlockSpec(memory_space=pltpu.SMEM)


def shape(dims, kind):
    return jax.ShapeDtypeStruct(dims, kind)


def params(mib):
    return pltpu.CompilerParams(vmem_limit_bytes=mib * MIB)


def on_device(
    row_count, col_count, design, active, stamp_basis, film_field, lift_weight, lift_bias,
    conv_weight, conv_bias, readout, target, dilation,
):
    grid = (row_count, col_count)
    here = jnp.stack([lax.axis_index("rows"), lax.axis_index("cols")]).astype(jnp.int32)
    place = jnp.concatenate([here, dilation])
    one, two, three = pl.pallas_call(
        pack_kernel,
        out_shape=(shape((39, 16, TC), bf16), shape((33, 16, TC), bf16), shape((1, 16, TC), bf16)),
        in_specs=[pl.BlockSpec(memory_space=pltpu.HBM)] * 4,
        out_specs=(vmem(),) * 3,
        scratch_shapes=[
            pltpu.VMEM(film_field.shape, bf16),
            pltpu.VMEM(design.shape, f32),
            pltpu.VMEM(active.shape, jnp.int32),
            pltpu.VMEM(target.shape, f32),
            pltpu.SemaphoreType.DMA((4,)),
        ],
        compiler_params=params(8),
        name="pack",
    )(*[pltpu.with_memory_space_constraint(x, pltpu.HBM) for x in (film_field, design, active, target)])

    def shifted(x, axis, by):
        count = lax.axis_size(axis)
        return lax.ppermute(x, axis, [(i, (i + by) % count) for i in range(count)])

    u1, d1 = shifted(one, "rows", 1), shifted(one, "rows", -1)
    u2, d2 = shifted(two, "rows", 2), shifted(two, "rows", -2)

    s2, expand = pl.pallas_call(
        prep_kernel,
        out_shape=(shape((2, NP * 32, WIDE), f32), shape((2, 384, WIDE), bf16)),
        in_specs=[vmem()],
        out_specs=(vmem(), vmem()),
        compiler_params=params(8),
        name="prep",
    )(stamp_basis.reshape(NP * 32, 32))
    def far(x):
        return shifted(x, "rows", 3), shifted(x, "rows", -3)

    def near(x):
        return jnp.zeros_like(x), jnp.zeros_like(x)

    later, s2, expand = lax.optimization_barrier((dilation, s2, expand))
    amps3 = jnp.concatenate(
        lax.cond(2 * jnp.sum(later) > HALO - HALF, far, near, three), axis=0
    )
    def paired(w):
        return jnp.concatenate(
            [jnp.pad(w, ((0, 0), (0, 0), (0, 48))), jnp.pad(w, ((0, 0), (0, 0), (48, 0)))], axis=1
        )

    wf = jnp.transpose(conv_weight, (0, 2, 1, 3)).reshape(LAYERS, 16, 144)
    wb = jnp.transpose(conv_weight[:, ::-1], (0, 3, 1, 2)).reshape(LAYERS, 16, 144)
    vec = jnp.concatenate(
        [lift_weight[None], lift_bias[None], readout[None], conv_bias], axis=0
    )[:, :, None]
    u1, d1, u2, d2, amps3, place = lax.optimization_barrier((u1, d1, u2, d2, amps3, place))
    tiles = (one, u1, u2, d1, d2, amps3)
    to_right, to_left = pl.pallas_call(
        halve_kernel,
        out_shape=(shape((SIDES, 16, TC), bf16),) * 2,
        in_specs=[vmem()] * 6,
        out_specs=(vmem(),) * 2,
        compiler_params=params(8),
        name="halve",
    )(*tiles)
    from_left = shifted(to_right, "cols", 1)
    from_right = shifted(to_left, "cols", -1)
    scratch = [
        pltpu.VMEM((SPARE + 1, 48, WIDE), bf16),
        pltpu.VMEM((SPARE + 1, 48, WIDE), bf16),
        pltpu.VMEM((LAYERS - 1, ROWS, 16, WIDE), f32),
        pltpu.VMEM((ROWS, 16, WIDE), f32),
        pltpu.VMEM((ROWS, WIDE), f32),
        pltpu.VMEM((TR + HALF, WIDE), f32),
        pltpu.VMEM((2, 112, WIDE), f32),
        pltpu.VMEM((ROWS, WIDE), f32),
    ]
    common = (place, vec, paired(wf), paired(wb), s2, expand, *tiles, from_left, from_right)
    specs = [smem()] + [vmem()] * 13

    def gather(message):
        return lax.all_to_all(message, ("rows", "cols"), 0, 0)

    devices = row_count * col_count
    message_shape = shape((devices, 1, 2 * TC), f32)

    message1 = pl.pallas_call(
        functools.partial(step_kernel, False, grid),
        out_shape=message_shape,
        in_specs=specs,
        out_specs=vmem(),
        scratch_shapes=scratch,
        compiler_params=params(30),
        name="step_one",
    )(*common)
    gathered1 = gather(message1)
    message2, moved = pl.pallas_call(
        functools.partial(step_kernel, True, grid),
        out_shape=(message_shape, shape((1, TC), f32)),
        in_specs=specs + [vmem()],
        out_specs=(vmem(), vmem()),
        scratch_shapes=[pltpu.VMEM((devices, TC), f32)] + scratch,
        compiler_params=params(30),
        name="step_two",
    )(*common, gathered1)
    gathered2 = gather(message2)
    new_design, objective = pl.pallas_call(
        functools.partial(final_kernel, grid),
        out_shape=(shape((NP, 2, HALF), f32), shape((2,), f32)),
        in_specs=[smem()] + [vmem()] * 3,
        out_specs=(vmem(), smem()),
        scratch_shapes=[pltpu.VMEM((devices, TC), f32)],
        compiler_params=params(8),
        name="finish",
    )(place, design, gathered2, moved)
    return new_design, objective


def solution(mesh):
    placed = (
        P(None, "rows", "cols"),
        P("rows", "cols"),
        P(),
        P(None, "rows", "cols"),
        P(),
        P(),
        P(),
        P(),
        P(),
        P("rows", "cols"),
        P(),
    )
    return jax.shard_map(
        functools.partial(on_device, mesh.shape["rows"], mesh.shape["cols"]),
        mesh=mesh,
        in_specs=placed,
        out_specs=(P(None, "rows", "cols"), P()),
        check_vma=False,
    )
```

```python
import functools

import jax
import jax.numpy as jnp
import numpy as np
from jax import lax
from jax.experimental import pallas as pl
from jax.experimental.pallas import tpu as pltpu
from jax.sharding import PartitionSpec as P

f32 = jnp.float32
bf16 = jnp.bfloat16
step_rate = 0.25
norm_eps = 1e-06

NP = 6
LAYERS = 4
SIDE = 16
HALF = 8
TR = 32
TC = 128
HALO = 64
WIDE = TC + 2 * HALO
ROWS = TR + 2 * HALO
SPARE = ROWS + 16
PAIRS = 16
MIB = 1024 * 1024


def iota(shape, dim):
    return lax.broadcasted_iota(jnp.int32, shape, dim)


def cell_col(dims):
    lane = iota(dims, 1)
    return jnp.where(lane < TC + HALO, lane, lane - WIDE)


def split3(x):
    hi = x.astype(bf16)
    rest = x - hi.astype(f32)
    mid = rest.astype(bf16)
    low = (rest - mid.astype(f32)).astype(bf16)
    return hi, mid, low


def dot(a, b):
    return jnp.dot(a, b, preferred_element_type=f32)


def exact_dot(x, ones):
    hi, mid, low = split3(x)
    return dot(hi, ones) + dot(mid, ones) + dot(low, ones)


def lane_fields(width):
    lane = iota((1, width), 1) % 128
    group = lane // 10
    return group, lane - 10 * group, lane < 120


def pack_kernel(
    film_hbm, design_hbm, active_hbm, target_hbm, one_ref, two_ref, three_ref,
    film_ref, design_ref, active_ref, target_ref, sems,
):
    reads = [
        pltpu.make_async_copy(src, dst, sems.at[n])
        for n, (src, dst) in enumerate(
            (
                (design_hbm, design_ref),
                (active_hbm, active_ref),
                (target_hbm, target_ref),
                (film_hbm, film_ref),
            )
        )
    ]
    for read in reads:
        read.start()
    for read in reads:
        read.wait()
    group, spot, used = lane_fields(TC)
    spread = jnp.where(
        (iota((HALF, TC), 0) == spot - 1) & used, 1.0, 0.0
    ).astype(bf16)
    active = active_ref[...].astype(f32)
    row_of = iota((2, TC), 0)
    amp_row = jnp.zeros((1, TC), f32)
    act_row = jnp.zeros((1, TC), f32)
    act_spread = exact_dot(active, spread)
    for p in range(NP):
        mine = row_of + 2 * p == group
        placed = jnp.where(mine, exact_dot(design_ref[p] * active, spread), 0.0)
        amp_row = amp_row + jnp.sum(placed, axis=0, keepdims=True)
        act_row = act_row + jnp.sum(jnp.where(mine, act_spread, 0.0), axis=0, keepdims=True)
    hi, mid, low = split3(amp_row)
    sub = iota((16, TC), 0)
    tile = jnp.where(sub == 0, hi.astype(f32), 0.0)
    tile = jnp.where(sub == 1, mid.astype(f32), tile)
    tile = jnp.where(sub == 2, low.astype(f32), tile)
    tile = jnp.where(sub == 3, act_row, tile).astype(bf16)
    one_ref[0] = tile
    two_ref[0] = tile
    three_ref[0] = tile
    film = jnp.swapaxes(film_ref[...].astype(f32), 0, 1).astype(bf16)
    one_ref[1 : 1 + TR] = film
    two_ref[1 : 1 + TR] = film
    for n, piece in enumerate(split3(target_ref[...])):
        one_ref[33 + 2 * n] = piece[:16]
        one_ref[34 + 2 * n] = piece[16:]


SIDES = 96
AMPS = 89


def tile_pairs(u2, u1, own, d1, d2):
    pairs = [((u2, 1 + r), (u1, 1 + r)) for r in range(TR)]
    pairs += [((own, 1 + r), (own, 17 + r)) for r in range(16)]
    pairs += [((d1, 1 + r), (d2, 1 + r)) for r in range(TR)]
    pairs += [((u1, 33 + r), (d1, 33 + r)) for r in range(6)]
    return pairs + [((own, 33 + r), (own, 36 + r)) for r in range(3)]


def amp_tiles(u2, u1, own, d1, d2, far):
    return (far, 0), (u2, 0), (u1, 0), (own, 0), (d1, 0), (d2, 0), (far, 1)


def swap_halves(x):
    return pltpu.roll(x, TC // 2, 1)


def halve_kernel(
    own_ref, u1_ref, u2_ref, d1_ref, d2_ref, far_ref, right_ref, left_ref
):
    low_half = iota((16, TC), 1) < HALO
    pairs = tile_pairs(u2_ref, u1_ref, own_ref, d1_ref, d2_ref)
    for n, ((ref_a, a), (ref_b, b)) in enumerate(pairs):
        first, second = ref_a[a].astype(f32), ref_b[b].astype(f32)
        right_ref[n] = jnp.where(low_half, swap_halves(first), second).astype(bf16)
        left_ref[n] = jnp.where(low_half, first, swap_halves(second)).astype(bf16)
    amps = amp_tiles(u2_ref, u1_ref, own_ref, d1_ref, d2_ref, far_ref)
    for n, (ref, at) in enumerate(amps):
        right_ref[AMPS + n] = ref[at]
        left_ref[AMPS + n] = ref[at]


def combine(gathered):
    own, ring = gathered[:, :128], gathered[:, 128:]
    group, spot, used = lane_fields(128)
    top = (group % 2 == 0) & used
    bottom = (group % 2 == 1) & used
    zero = jnp.zeros((16, 128), f32)
    above = jnp.concatenate([zero, ring[:240]], axis=0)
    below = jnp.concatenate([ring[16:], zero], axis=0)
    summed = own + jnp.where(top, above, 0.0) + jnp.where(bottom, below, 0.0)
    place = iota((256, 128), 0) % 16
    left = jnp.where(place == 0, 0.0, pltpu.roll(summed, 1, 0))
    right = jnp.where(place == 15, 0.0, pltpu.roll(summed, 255, 0))
    left = pltpu.roll(left, 120, 1)
    right = pltpu.roll(right, 8, 1)
    whole = summed + jnp.where(spot == 1, left, 0.0) + jnp.where(spot == 8, right, 0.0)
    whole = jnp.where((spot >= 1) & (spot <= 8) & used, whole, 0.0)
    squares = jnp.sum(jnp.sum(whole * whole, axis=0, keepdims=True), axis=1, keepdims=True)
    lane = iota((1, 128), 1)
    misfits = jnp.sum(
        jnp.where(lane == 120, jnp.sum(own, axis=0, keepdims=True), 0.0), axis=1, keepdims=True
    )
    return whole, squares, misfits


def rate_of(squares, entries):
    return step_rate / jnp.sqrt(squares / entries + norm_eps)


def prep_kernel(stamp_ref, s2_ref, expand_ref):
    for k in range(2):
        pick = jnp.where(
            iota((32, WIDE), 0) == (iota((32, WIDE), 1) + HALF) % SIDE + SIDE * k, 1.0, 0.0
        ).astype(bf16)
        s2_ref[k] = exact_dot(stamp_ref[...], pick)
    lane3 = iota((384, WIDE), 0)
    lane1 = lane3 % 128
    spot3 = lane1 % 10
    for k in range(2):
        b = (cell_col((384, WIDE)) + HALO + HALF) // SIDE - HALO // SIDE - k
        hit = (b == HALF * (lane3 // 128 - 1) + spot3 - 1) & (spot3 >= 1) & (spot3 <= 8)
        expand_ref[k] = jnp.where(hit & (lane1 < 120), 1.0, 0.0).astype(bf16)


def step_kernel(second, grid, *refs):
    row_count, col_count = grid
    (place_ref, vec_ref, wf_ref, wb_ref, s2_ref, expand_ref, own_ref, u1_ref, u2_ref,
     d1_ref, d2_ref, far_ref, from_left_ref, from_right_ref) = refs[:14]
    rest = refs[14:]
    if second:
        gathered_ref, out_ref, moved_ref, whole_ref = rest[:4]
        rest = rest[4:]
    else:
        out_ref, rest = rest[0], rest[1:]
    cat0_ref, cat1_ref, sp_ref, adj_ref, height_ref, hg_ref, ampx_ref, acc_ref = rest
    my_row = place_ref[0]
    my_col = place_ref[1]
    group, spot, used = lane_fields(128)
    amps = amp_tiles(u2_ref, u1_ref, own_ref, d1_ref, d2_ref, far_ref)

    if second:
        whole, squares, misfits = combine(gathered_ref[...].reshape(row_count * col_count, 2 * TC))
        whole_ref[...] = whole
        rate = rate_of(squares, float(row_count * col_count * NP * 16))
    masks = iota((16, 384), 0) == jnp.concatenate([group] * 3, axis=1)
    acts = {}
    stacked = []
    for dr in range(-3, 4):
        ref, at = amps[dr + 3]
        tiles = [from_left_ref[AMPS + dr + 3], ref[at], from_right_ref[AMPS + dr + 3]]
        pieces = []
        for dc, tile in zip((-1, 0, 1), tiles):
            t = tile.astype(f32)
            r, c = my_row + dr, my_col + dc
            inside = (r >= 0) & (r < row_count) & (c >= 0) & (c < col_count)
            t = t * jnp.where(inside, 1.0, 0.0)
            amp = t[0:1] + t[1:2] + t[2:3]
            if second:
                dev = jnp.where(inside, r * col_count + c, 0)
                moved = rate * whole_ref[pl.ds(dev, 1), :]
                moved = moved * jnp.where(inside, 1.0, 0.0)
                if dr == 0 and dc == 0:
                    moved_ref[...] = jnp.where(iota((1, TC), 1) == 120, misfits, moved)
                amp = amp - moved
            pieces.append(amp)
            acts[dr, dc] = t[3:4]
        row = jnp.concatenate(pieces, axis=1)
        stacked.append(jnp.where(masks, row, 0.0))
    stacked = jnp.concatenate(stacked, axis=0)
    for k in range(2):
        ampx_ref[k] = exact_dot(stacked, expand_ref[k])

    blocks = range(-4, 6)
    for half in range(2):
        totals = [jnp.zeros((HALF, WIDE), f32) for _ in blocks]
        for step, first in ((0, 16 * half if half else 8), (1 if half else -1, 0 if half else 24)):
            for p in range(NP):
                for k in range(2):
                    stamp = s2_ref[k, 32 * p + first : 32 * p + first + HALF, :]
                    for n, a in enumerate(blocks):
                        dr, i = (a + step) // 2, (a + step) % 2
                        row = 16 * (dr + 3) + 2 * p + i
                        totals[n] = totals[n] + stamp * ampx_ref[k, row : row + 1, :]
        for n, a in enumerate(blocks):
            start = HALO + SIDE * a + HALF * half
            height_ref[start : start + HALF, :] = totals[n]

    col = my_col * TC + cell_col((16, WIDE))
    in_map = (col >= 0) & (col < col_count * TC)

    cats = (cat0_ref, cat1_ref)

    def put(slot, b, value, shift):
        cat = cats[slot]
        b = jnp.where(b < map_hi, b, SPARE)
        value = jnp.where(in_map, value, 0.0)
        cat[b, 16:32, :] = value.astype(bf16)
        cat[b, 0:16, :] = pltpu.roll(value, shift, 1).astype(bf16)
        cat[b, 32:48, :] = pltpu.roll(value, WIDE - shift, 1).astype(bf16)

    def wide_row(ref):
        return jnp.broadcast_to(ref, (16, WIDE))

    lift_w = wide_row(vec_ref[0])
    map_lo = jnp.maximum(0, HALO - my_row * TR)
    map_hi = jnp.minimum(ROWS, HALO + (row_count - my_row) * TR)
    d = [place_ref[2 + l] for l in range(LAYERS)]
    total_d = d[0] + d[1] + d[2] + d[3]

    def bounds(reach):
        return jnp.maximum(map_lo, HALO - reach), jnp.minimum(map_hi, HALO + TR + reach)

    def over(lo, hi, dil, some_pairs):
        count = hi - lo
        whole = count // (2 * dil)
        pairs = whole * dil + jnp.minimum(dil, count - whole * 2 * dil)

        def some(number, base, i):
            firsts = []
            for _ in range(number):
                firsts.append(base + i)
                wrap = i + 1 >= dil
                next_base = jnp.where(wrap, base + 2 * dil, base)
                next_i = jnp.where(wrap, 0, i + 1)
                inside = next_base + next_i < hi
                base = jnp.where(inside, next_base, base)
                i = jnp.where(inside, next_i, i)
            some_pairs(firsts)
            return base, i

        full = pairs // PAIRS
        rest = pairs - PAIRS * full
        full = full + jnp.where(rest > PAIRS // 2, 1, 0)
        base, i = lax.fori_loop(
            0, full, lambda step, at: some(PAIRS, *at), (lo, jnp.int32(0))
        )

        @pl.when((rest > 0) & (rest <= PAIRS // 2))
        def _():
            some(PAIRS // 2, base, i)

    lo0, hi0 = bounds(2 * total_d)
    lift_b = wide_row(vec_ref[1])
    low_half = iota((16, TC), 1) < HALO

    def beside(place, second_row):
        left = from_left_ref[place].astype(f32)
        right = from_right_ref[place].astype(f32)
        if second_row:
            right = swap_halves(right)
        else:
            left = swap_halves(left)
        return jnp.where(low_half, right, left)

    spans = (
        (0, u2_ref, 0, TR, 0, False),
        (1, u1_ref, 0, TR, 0, True),
        (2, own_ref, 0, 16, 32, False),
        (2, own_ref, 16, 16, 32, True),
        (3, d1_ref, 0, TR, 48, False),
        (4, d2_ref, 0, TR, 48, True),
    )
    for n, ref, row0, count, place, second_row in spans:
        here = my_row + n - 2
        valid = (here >= 0) & (here < row_count)
        start = n * TR + row0
        first = jnp.clip(lo0 - start, 0, count)
        after = jnp.clip(hi0 - start, 0, count)

        def rows(step, _):
            r0 = jnp.minimum(first + step * 16, count - 16)
            hs = [height_ref[pl.ds(start + r0 + q, 1), :] for q in range(16)]
            for q in range(16):
                film = jnp.concatenate(
                    [
                        ref[1 + row0 + r0 + q].astype(f32),
                        beside(place + r0 + q, second_row),
                    ],
                    axis=1,
                )
                value = (lift_w * hs[q] + lift_b + film).astype(bf16).astype(f32)
                put(0, start + r0 + q, value, d[0])
            return 0

        lax.fori_loop(0, (after - first + 15) // 16, rows, 0)

        @pl.when(jnp.logical_not(valid))
        def _():
            def blank(r, _):
                cat0_ref[start + r] = jnp.zeros((48, WIDE), bf16)
                cat1_ref[start + r] = jnp.zeros((48, WIDE), bf16)
                return 0

            lax.fori_loop(0, count, blank, 0)

    def convs(w, slot, firsts, dil):
        cat = cats[slot]
        rows, sums = [], []
        for r in firsts:
            near = [cat[r - dil], cat[r], cat[r + dil], cat[r + 2 * dil]]
            both = dot(w, jnp.concatenate(near, axis=0))
            rows += [r, r + dil]
            sums += [both[:16], both[16:]]
        return rows, sums

    def parts(pre):
        s = 0.5 + 0.5 * jnp.tanh(0.5 * pre)
        silu = pre * s
        return silu, s + silu * (1.0 - s)

    reach = 2 * total_d
    for l in range(LAYERS - 1):
        slot = l % 2
        w = wf_ref[l]
        bias = wide_row(vec_ref[3 + l])
        reach = reach - d[l]
        lo, hi = bounds(reach)

        def forward(firsts):
            for b, pre in zip(*convs(w, slot, firsts, d[l])):
                silu, slope = parts(pre + bias)
                sp_ref[l, b] = slope
                value = cats[slot][b, 16:32, :].astype(f32) + silu
                put(1 - slot, b, value.astype(bf16).astype(f32), d[l + 1])

        over(lo, hi, d[l], forward)

    sides = (
        [(80 + r, False) for r in range(6)],
        [(86 + r % 3, r >= 3) for r in range(6)],
        [(80 + r, True) for r in range(6)],
    )
    for n, ref in enumerate((u1_ref, own_ref, d1_ref)):
        for half in range(2):
            target, side = jnp.zeros((16, TC), f32), jnp.zeros((16, TC), f32)
            for piece in (half, half + 2, half + 4):
                target = target + ref[33 + piece].astype(f32)
                side = side + beside(*sides[n][piece])
            first = TR * (n + 1) + 16 * half
            height_ref[first : first + 16, :TC] = target
            height_ref[first : first + 16, TC:] = side

    acc_ref[...] = jnp.zeros_like(acc_ref)
    lo, hi = bounds(total_d)
    w3 = wf_ref[3]
    bias3 = wide_row(vec_ref[6])
    readout = wide_row(vec_ref[2])

    def turn(firsts):
        rows, pres = convs(w3, 1, firsts, d[3])
        targets = [height_ref[pl.ds(b, 1), :] for b in rows]
        for b, pre, target in zip(rows, pres, targets):
            silu, slope = parts(pre + bias3)
            value = (cat1_ref[b, 16:32, :].astype(f32) + silu).astype(bf16).astype(f32)
            pressure = jnp.sum(readout * value, axis=0, keepdims=True)
            misfit = pressure - target
            acc_ref[pl.ds(b, 1), :] = misfit * misfit
            adj = readout * (misfit * (1.0 / (SIDE * SIDE)))
            adj_ref[b] = adj
            put(0, b, (adj * slope).astype(bf16).astype(f32), d[3])

    over(lo, hi, d[3], turn)

    reach = total_d
    for l in range(LAYERS - 1, 0, -1):
        slot = (l + 1) % 2
        wb = wb_ref[l]
        reach = reach - d[l]
        lo, hi = bounds(reach)

        def backward(firsts):
            rows, sums = convs(wb, slot, firsts, d[l])
            olds = [adj_ref[b] for b in rows]
            for b, old, change in zip(rows, olds, sums):
                adj = old + change
                adj_ref[b] = adj
                put(1 - slot, b, (adj * sp_ref[l - 1, b]).astype(bf16).astype(f32), d[l - 1])

        over(lo, hi, d[l], backward)

    w0 = wb_ref[0]

    def last(firsts):
        rows, sums = convs(w0, 1, firsts, d[0])
        for b, change in zip(rows, sums):
            adj = adj_ref[b] + change
            hg_ref[pl.ds(b - HALO, 1), :] = jnp.sum(lift_w * adj, axis=0, keepdims=True)

    over(jnp.int32(HALO), jnp.int32(HALO + TR), d[0], last)

    hg = hg_ref[:TR, :TC]
    spans = {-1: (0, 8, 24), 0: (0, 24, 8), 1: (8, 32, 0), 2: (24, 32, 0)}
    message = []
    for block in ((0, 1), (2, -1)):
        lanes = jnp.zeros((1, TC), f32)
        for k in range(2):
            rows = []
            for p in range(NP):
                for dimple in block:
                    lo_r, hi_r, first = spans[dimple]
                    n = hi_r - lo_r
                    prod = hg[lo_r:hi_r] * s2_ref[k, 32 * p + first : 32 * p + first + n, :TC]
                    rows.append(jnp.sum(prod, axis=0, keepdims=True))
            rows += [jnp.zeros((4, TC), f32)]
            sums = jnp.concatenate(rows, axis=0)
            c = iota((TC, TC), 0)
            gather = jnp.where(((c + HALF) // SIDE - k + 1 == spot) & used, 1.0, 0.0)
            z = exact_dot(sums, gather.astype(bf16))
            lanes = lanes + jnp.sum(
                jnp.where(iota((16, TC), 0) == group, z, 0.0), axis=0, keepdims=True
            )
        message.append(lanes)

    def act_ext(dr):
        act = acts[dr, 0]
        act = act + jnp.where(spot == 0, pltpu.roll(acts[dr, -1], 120, 1), 0.0)
        return act + jnp.where(spot == 9, pltpu.roll(acts[dr, 1], 8, 1), 0.0)

    lane = iota((1, TC), 1)
    own_act = act_ext(0)
    ring_act = jnp.where(group % 2 == 0, act_ext(1), act_ext(-1))
    acc = jnp.sum(acc_ref[HALO : HALO + TR, :], axis=0, keepdims=True)
    local = 0.5 * jnp.sum(acc[:, :TC], axis=1, keepdims=True)
    first = jnp.where(used, message[0] * own_act, jnp.where(lane == 120, local, 0.0))
    ring = jnp.where(used, message[1] * ring_act, 0.0)
    whole_message = jnp.concatenate([first, ring], axis=1)
    out_ref[...] = jnp.broadcast_to(whole_message[None], out_ref.shape)


def final_kernel(grid, place_ref, design_ref, gathered2_ref, moved_ref, new_ref, obj_ref, whole_ref):
    row_count, col_count = grid
    whole, squares, misfit2 = combine(gathered2_ref[...].reshape(row_count * col_count, 2 * TC))
    lane = iota((1, 128), 1)
    whole_ref[...] = whole
    entries = float(row_count * col_count * NP * 16)
    cells = float(row_count * col_count * TR * TC)
    dev = place_ref[0] * col_count + place_ref[1]
    moved = moved_ref[...] + rate_of(squares, entries) * whole_ref[pl.ds(dev, 1), :]
    group, _, _ = lane_fields(128)
    by_group = jnp.where(iota((16, 128), 0) == group, moved, 0.0)
    lanes = iota((128, HALF), 0)
    pick = jnp.where((lanes % 10 == iota((128, HALF), 1) + 1) & (lanes < 120), 1.0, 0.0)
    change = exact_dot(by_group, pick.astype(bf16))
    for p in range(NP):
        new_ref[p] = design_ref[p] - change[2 * p : 2 * p + 2]
    misfit1 = jnp.sum(jnp.where(lane == 120, moved_ref[...], 0.0), axis=1, keepdims=True)
    obj_ref[0] = jnp.sum(misfit1) / cells
    obj_ref[1] = jnp.sum(misfit2) / cells


def vmem():
    return pl.BlockSpec(memory_space=pltpu.VMEM)


def smem():
    return pl.BlockSpec(memory_space=pltpu.SMEM)


def shape(dims, kind):
    return jax.ShapeDtypeStruct(dims, kind)


def params(mib):
    return pltpu.CompilerParams(vmem_limit_bytes=mib * MIB)


def on_device(
    row_count, col_count, design, active, stamp_basis, film_field, lift_weight, lift_bias,
    conv_weight, conv_bias, readout, target, dilation,
):
    grid = (row_count, col_count)
    here = jnp.stack([lax.axis_index("rows"), lax.axis_index("cols")]).astype(jnp.int32)
    place = jnp.concatenate([here, dilation])
    one, two, three = pl.pallas_call(
        pack_kernel,
        out_shape=(shape((39, 16, TC), bf16), shape((33, 16, TC), bf16), shape((1, 16, TC), bf16)),
        in_specs=[pl.BlockSpec(memory_space=pltpu.HBM)] * 4,
        out_specs=(vmem(),) * 3,
        scratch_shapes=[
            pltpu.VMEM(film_field.shape, bf16),
            pltpu.VMEM(design.shape, f32),
            pltpu.VMEM(active.shape, jnp.int32),
            pltpu.VMEM(target.shape, f32),
            pltpu.SemaphoreType.DMA((4,)),
        ],
        compiler_params=params(8),
        name="pack",
    )(*[pltpu.with_memory_space_constraint(x, pltpu.HBM) for x in (film_field, design, active, target)])

    def shifted(x, axis, by):
        count = lax.axis_size(axis)
        return lax.ppermute(x, axis, [(i, (i + by) % count) for i in range(count)])

    u1, d1 = shifted(one, "rows", 1), shifted(one, "rows", -1)
    u2, d2 = shifted(two, "rows", 2), shifted(two, "rows", -2)

    s2, expand = pl.pallas_call(
        prep_kernel,
        out_shape=(shape((2, NP * 32, WIDE), f32), shape((2, 384, WIDE), bf16)),
        in_specs=[vmem()],
        out_specs=(vmem(), vmem()),
        compiler_params=params(8),
        name="prep",
    )(stamp_basis.reshape(NP * 32, 32))
    def far(x):
        return jnp.concatenate([shifted(x, "rows", 3), shifted(x, "rows", -3)], axis=0)

    def near(x):
        return jnp.zeros((2, 16, TC), bf16)

    later, d2 = lax.optimization_barrier((dilation, d2))
    amps3 = lax.cond(2 * jnp.sum(later) > HALO - HALF, far, near, three)

    def paired(w):
        return jnp.concatenate(
            [jnp.pad(w, ((0, 0), (0, 0), (0, 48))), jnp.pad(w, ((0, 0), (0, 0), (48, 0)))], axis=1
        )

    wf = jnp.transpose(conv_weight, (0, 2, 1, 3)).reshape(LAYERS, 16, 144)
    wb = jnp.transpose(conv_weight[:, ::-1], (0, 3, 1, 2)).reshape(LAYERS, 16, 144)
    vec = jnp.concatenate(
        [lift_weight[None], lift_bias[None], readout[None], conv_bias], axis=0
    )[:, :, None]
    u1, d1, u2, d2, amps3, place, s2, expand = lax.optimization_barrier(
        (u1, d1, u2, d2, amps3, place, s2, expand)
    )
    tiles = (one, u1, u2, d1, d2, amps3)
    to_right, to_left = pl.pallas_call(
        halve_kernel,
        out_shape=(shape((SIDES, 16, TC), bf16),) * 2,
        in_specs=[vmem()] * 6,
        out_specs=(vmem(),) * 2,
        compiler_params=params(8),
        name="halve",
    )(*tiles)
    from_left = shifted(to_right, "cols", 1)
    from_right = shifted(to_left, "cols", -1)
    scratch = [
        pltpu.VMEM((SPARE + 1, 48, WIDE), bf16),
        pltpu.VMEM((SPARE + 1, 48, WIDE), bf16),
        pltpu.VMEM((LAYERS - 1, ROWS, 16, WIDE), f32),
        pltpu.VMEM((ROWS, 16, WIDE), f32),
        pltpu.VMEM((ROWS, WIDE), f32),
        pltpu.VMEM((TR + HALF, WIDE), f32),
        pltpu.VMEM((2, 112, WIDE), f32),
        pltpu.VMEM((ROWS, WIDE), f32),
    ]
    common = (place, vec, paired(wf), paired(wb), s2, expand, *tiles, from_left, from_right)
    specs = [smem()] + [vmem()] * 13

    def gather(message):
        return lax.all_to_all(message, ("rows", "cols"), 0, 0)

    devices = row_count * col_count
    message_shape = shape((devices, 1, 2 * TC), f32)

    message1 = pl.pallas_call(
        functools.partial(step_kernel, False, grid),
        out_shape=message_shape,
        in_specs=specs,
        out_specs=vmem(),
        scratch_shapes=scratch,
        compiler_params=params(30),
        name="step_one",
    )(*common)
    gathered1 = gather(message1)
    message2, moved = pl.pallas_call(
        functools.partial(step_kernel, True, grid),
        out_shape=(message_shape, shape((1, TC), f32)),
        in_specs=specs + [vmem()],
        out_specs=(vmem(), vmem()),
        scratch_shapes=[pltpu.VMEM((devices, TC), f32)] + scratch,
        compiler_params=params(30),
        name="step_two",
    )(*common, gathered1)
    gathered2 = gather(message2)
    new_design, objective = pl.pallas_call(
        functools.partial(final_kernel, grid),
        out_shape=(shape((NP, 2, HALF), f32), shape((2,), f32)),
        in_specs=[smem()] + [vmem()] * 3,
        out_specs=(vmem(), smem()),
        scratch_shapes=[pltpu.VMEM((devices, TC), f32)],
        compiler_params=params(8),
        name="finish",
    )(place, design, gathered2, moved)
    return new_design, objective


def solution(mesh):
    placed = (
        P(None, "rows", "cols"),
        P("rows", "cols"),
        P(),
        P(None, "rows", "cols"),
        P(),
        P(),
        P(),
        P(),
        P(),
        P("rows", "cols"),
        P(),
    )
    return jax.shard_map(
        functools.partial(on_device, mesh.shape["rows"], mesh.shape["cols"]),
        mesh=mesh,
        in_specs=placed,
        out_specs=(P(None, "rows", "cols"), P()),
        check_vma=False,
    )
```

```python
import functools

import jax
import jax.numpy as jnp
import numpy as np
from jax import lax
from jax.experimental import pallas as pl
from jax.experimental.pallas import tpu as pltpu
from jax.sharding import PartitionSpec as P

f32 = jnp.float32
bf16 = jnp.bfloat16
step_rate = 0.25
norm_eps = 1e-06

NP = 6
LAYERS = 4
SIDE = 16
HALF = 8
TR = 32
TC = 128
HALO = 64
WIDE = TC + 2 * HALO
ROWS = TR + 2 * HALO
SPARE = ROWS + 16
PAIRS = 16
MIB = 1024 * 1024


def iota(shape, dim):
    return lax.broadcasted_iota(jnp.int32, shape, dim)


def cell_col(dims):
    lane = iota(dims, 1)
    return jnp.where(lane < TC + HALO, lane, lane - WIDE)


def split3(x):
    hi = x.astype(bf16)
    rest = x - hi.astype(f32)
    mid = rest.astype(bf16)
    low = (rest - mid.astype(f32)).astype(bf16)
    return hi, mid, low


def dot(a, b):
    return jnp.dot(a, b, preferred_element_type=f32)


def exact_dot(x, ones):
    hi, mid, low = split3(x)
    return dot(hi, ones) + dot(mid, ones) + dot(low, ones)


def lane_fields(width):
    lane = iota((1, width), 1) % 128
    group = lane // 10
    return group, lane - 10 * group, lane < 120


def pack_kernel(
    film_hbm, design_hbm, active_hbm, target_hbm, one_ref, two_ref, three_ref,
    film_ref, design_ref, active_ref, target_ref, sems,
):
    reads = [
        pltpu.make_async_copy(src, dst, sems.at[n])
        for n, (src, dst) in enumerate(
            (
                (design_hbm, design_ref),
                (active_hbm, active_ref),
                (target_hbm, target_ref),
                (film_hbm, film_ref),
            )
        )
    ]
    for read in reads:
        read.start()
    for read in reads:
        read.wait()
    group, spot, used = lane_fields(TC)
    spread = jnp.where(
        (iota((HALF, TC), 0) == spot - 1) & used, 1.0, 0.0
    ).astype(bf16)
    active = active_ref[...].astype(f32)
    row_of = iota((2, TC), 0)
    amp_row = jnp.zeros((1, TC), f32)
    act_row = jnp.zeros((1, TC), f32)
    act_spread = exact_dot(active, spread)
    for p in range(NP):
        mine = row_of + 2 * p == group
        placed = jnp.where(mine, exact_dot(design_ref[p] * active, spread), 0.0)
        amp_row = amp_row + jnp.sum(placed, axis=0, keepdims=True)
        act_row = act_row + jnp.sum(jnp.where(mine, act_spread, 0.0), axis=0, keepdims=True)
    hi, mid, low = split3(amp_row)
    sub = iota((16, TC), 0)
    tile = jnp.where(sub == 0, hi.astype(f32), 0.0)
    tile = jnp.where(sub == 1, mid.astype(f32), tile)
    tile = jnp.where(sub == 2, low.astype(f32), tile)
    tile = jnp.where(sub == 3, act_row, tile).astype(bf16)
    one_ref[0] = tile
    two_ref[0] = tile
    three_ref[0] = tile
    film = jnp.swapaxes(film_ref[...].astype(f32), 0, 1).astype(bf16)
    one_ref[1 : 1 + TR] = film
    two_ref[1 : 1 + TR] = film
    for n, piece in enumerate(split3(target_ref[...])):
        one_ref[33 + 2 * n] = piece[:16]
        one_ref[34 + 2 * n] = piece[16:]


SIDES = 96
AMPS = 89


def tile_pairs(u2, u1, own, d1, d2):
    pairs = [((u2, 1 + r), (u1, 1 + r)) for r in range(TR)]
    pairs += [((own, 1 + r), (own, 17 + r)) for r in range(16)]
    pairs += [((d1, 1 + r), (d2, 1 + r)) for r in range(TR)]
    pairs += [((u1, 33 + r), (d1, 33 + r)) for r in range(6)]
    return pairs + [((own, 33 + r), (own, 36 + r)) for r in range(3)]


def amp_tiles(u2, u1, own, d1, d2, far):
    return (far, 0), (u2, 0), (u1, 0), (own, 0), (d1, 0), (d2, 0), (far, 1)


def swap_halves(x):
    return pltpu.roll(x, TC // 2, 1)


def halve_kernel(
    own_ref, u1_ref, u2_ref, d1_ref, d2_ref, far_ref, right_ref, left_ref
):
    low_half = iota((16, TC), 1) < HALO
    pairs = tile_pairs(u2_ref, u1_ref, own_ref, d1_ref, d2_ref)
    for n, ((ref_a, a), (ref_b, b)) in enumerate(pairs):
        first, second = ref_a[a].astype(f32), ref_b[b].astype(f32)
        right_ref[n] = jnp.where(low_half, swap_halves(first), second).astype(bf16)
        left_ref[n] = jnp.where(low_half, first, swap_halves(second)).astype(bf16)
    amps = amp_tiles(u2_ref, u1_ref, own_ref, d1_ref, d2_ref, far_ref)
    for n, (ref, at) in enumerate(amps):
        right_ref[AMPS + n] = ref[at]
        left_ref[AMPS + n] = ref[at]


def combine(gathered):
    own, ring = gathered[:, :128], gathered[:, 128:]
    group, spot, used = lane_fields(128)
    top = (group % 2 == 0) & used
    bottom = (group % 2 == 1) & used
    zero = jnp.zeros((16, 128), f32)
    above = jnp.concatenate([zero, ring[:240]], axis=0)
    below = jnp.concatenate([ring[16:], zero], axis=0)
    summed = own + jnp.where(top, above, 0.0) + jnp.where(bottom, below, 0.0)
    place = iota((256, 128), 0) % 16
    left = jnp.where(place == 0, 0.0, pltpu.roll(summed, 1, 0))
    right = jnp.where(place == 15, 0.0, pltpu.roll(summed, 255, 0))
    left = pltpu.roll(left, 120, 1)
    right = pltpu.roll(right, 8, 1)
    whole = summed + jnp.where(spot == 1, left, 0.0) + jnp.where(spot == 8, right, 0.0)
    whole = jnp.where((spot >= 1) & (spot <= 8) & used, whole, 0.0)
    squares = jnp.sum(jnp.sum(whole * whole, axis=0, keepdims=True), axis=1, keepdims=True)
    lane = iota((1, 128), 1)
    misfits = jnp.sum(
        jnp.where(lane == 120, jnp.sum(own, axis=0, keepdims=True), 0.0), axis=1, keepdims=True
    )
    return whole, squares, misfits


def rate_of(squares, entries):
    return step_rate / jnp.sqrt(squares / entries + norm_eps)


def prep_kernel(stamp_ref, s2_ref, expand_ref):
    for k in range(2):
        pick = jnp.where(
            iota((32, WIDE), 0) == (iota((32, WIDE), 1) + HALF) % SIDE + SIDE * k, 1.0, 0.0
        ).astype(bf16)
        s2_ref[k] = exact_dot(stamp_ref[...], pick)
    lane3 = iota((384, WIDE), 0)
    lane1 = lane3 % 128
    spot3 = lane1 % 10
    for k in range(2):
        b = (cell_col((384, WIDE)) + HALO + HALF) // SIDE - HALO // SIDE - k
        hit = (b == HALF * (lane3 // 128 - 1) + spot3 - 1) & (spot3 >= 1) & (spot3 <= 8)
        expand_ref[k] = jnp.where(hit & (lane1 < 120), 1.0, 0.0).astype(bf16)


def step_kernel(second, grid, *refs):
    row_count, col_count = grid
    (place_ref, vec_ref, wf_ref, wb_ref, s2_ref, expand_ref, own_ref, u1_ref, u2_ref,
     d1_ref, d2_ref, far_ref, from_left_ref, from_right_ref) = refs[:14]
    rest = refs[14:]
    if second:
        gathered_ref, out_ref, moved_ref, whole_ref = rest[:4]
        rest = rest[4:]
    else:
        out_ref, rest = rest[0], rest[1:]
    cat0_ref, cat1_ref, sp_ref, adj_ref, height_ref, hg_ref, ampx_ref, acc_ref = rest
    my_row = place_ref[0]
    my_col = place_ref[1]
    group, spot, used = lane_fields(128)
    amps = amp_tiles(u2_ref, u1_ref, own_ref, d1_ref, d2_ref, far_ref)

    if second:
        whole, squares, misfits = combine(gathered_ref[...].reshape(row_count * col_count, 2 * TC))
        whole_ref[...] = whole
        rate = rate_of(squares, float(row_count * col_count * NP * 16))
    masks = iota((16, 384), 0) == jnp.concatenate([group] * 3, axis=1)
    acts = {}
    stacked = []
    for dr in range(-3, 4):
        ref, at = amps[dr + 3]
        tiles = [from_left_ref[AMPS + dr + 3], ref[at], from_right_ref[AMPS + dr + 3]]
        pieces = []
        for dc, tile in zip((-1, 0, 1), tiles):
            t = tile.astype(f32)
            r, c = my_row + dr, my_col + dc
            inside = (r >= 0) & (r < row_count) & (c >= 0) & (c < col_count)
            t = t * jnp.where(inside, 1.0, 0.0)
            amp = t[0:1] + t[1:2] + t[2:3]
            if second:
                dev = jnp.where(inside, r * col_count + c, 0)
                moved = rate * whole_ref[pl.ds(dev, 1), :]
                moved = moved * jnp.where(inside, 1.0, 0.0)
                if dr == 0 and dc == 0:
                    moved_ref[...] = jnp.where(iota((1, TC), 1) == 120, misfits, moved)
                amp = amp - moved
            pieces.append(amp)
            acts[dr, dc] = t[3:4]
        row = jnp.concatenate(pieces, axis=1)
        stacked.append(jnp.where(masks, row, 0.0))
    stacked = jnp.concatenate(stacked, axis=0)
    for k in range(2):
        ampx_ref[k] = exact_dot(stacked, expand_ref[k])

    blocks = range(-4, 6)
    for half in range(2):
        totals = [jnp.zeros((HALF, WIDE), f32) for _ in blocks]
        for step, first in ((0, 16 * half if half else 8), (1 if half else -1, 0 if half else 24)):
            for p in range(NP):
                for k in range(2):
                    stamp = s2_ref[k, 32 * p + first : 32 * p + first + HALF, :]
                    for n, a in enumerate(blocks):
                        dr, i = (a + step) // 2, (a + step) % 2
                        row = 16 * (dr + 3) + 2 * p + i
                        totals[n] = totals[n] + stamp * ampx_ref[k, row : row + 1, :]
        for n, a in enumerate(blocks):
            start = HALO + SIDE * a + HALF * half
            height_ref[start : start + HALF, :] = totals[n]

    col = my_col * TC + cell_col((16, WIDE))
    in_map = (col >= 0) & (col < col_count * TC)

    cats = (cat0_ref, cat1_ref)

    def put(slot, b, value, shift):
        cat = cats[slot]
        b = jnp.where(b < map_hi, b, SPARE)
        value = jnp.where(in_map, value, 0.0)
        cat[b, 16:32, :] = value.astype(bf16)
        cat[b, 0:16, :] = pltpu.roll(value, shift, 1).astype(bf16)
        cat[b, 32:48, :] = pltpu.roll(value, WIDE - shift, 1).astype(bf16)

    def wide_row(ref):
        return jnp.broadcast_to(ref, (16, WIDE))

    lift_w = wide_row(vec_ref[0])
    map_lo = jnp.maximum(0, HALO - my_row * TR)
    map_hi = jnp.minimum(ROWS, HALO + (row_count - my_row) * TR)
    d = [place_ref[2 + l] for l in range(LAYERS)]
    total_d = d[0] + d[1] + d[2] + d[3]

    def bounds(reach):
        return jnp.maximum(map_lo, HALO - reach), jnp.minimum(map_hi, HALO + TR + reach)

    def over(lo, hi, dil, some_pairs):
        count = hi - lo
        whole = count // (2 * dil)
        pairs = whole * dil + jnp.minimum(dil, count - whole * 2 * dil)

        def some(number, base, i):
            firsts = []
            for _ in range(number):
                firsts.append(base + i)
                wrap = i + 1 >= dil
                next_base = jnp.where(wrap, base + 2 * dil, base)
                next_i = jnp.where(wrap, 0, i + 1)
                inside = next_base + next_i < hi
                base = jnp.where(inside, next_base, base)
                i = jnp.where(inside, next_i, i)
            some_pairs(firsts)
            return base, i

        full = pairs // PAIRS
        rest = pairs - PAIRS * full
        full = full + jnp.where(rest > PAIRS // 2, 1, 0)
        base, i = lax.fori_loop(
            0, full, lambda step, at: some(PAIRS, *at), (lo, jnp.int32(0))
        )

        @pl.when((rest > 0) & (rest <= PAIRS // 2))
        def _():
            some(PAIRS // 2, base, i)

    lo0, hi0 = bounds(2 * total_d)
    lift_b = wide_row(vec_ref[1])
    low_half = iota((16, TC), 1) < HALO

    def beside(place, second_row):
        left = from_left_ref[place].astype(f32)
        right = from_right_ref[place].astype(f32)
        if second_row:
            right = swap_halves(right)
        else:
            left = swap_halves(left)
        return jnp.where(low_half, right, left)

    spans = (
        (0, u2_ref, 0, TR, 0, False),
        (1, u1_ref, 0, TR, 0, True),
        (2, own_ref, 0, 16, 32, False),
        (2, own_ref, 16, 16, 32, True),
        (3, d1_ref, 0, TR, 48, False),
        (4, d2_ref, 0, TR, 48, True),
    )
    for n, ref, row0, count, place, second_row in spans:
        here = my_row + n - 2
        valid = (here >= 0) & (here < row_count)
        start = n * TR + row0
        first = jnp.clip(lo0 - start, 0, count)
        after = jnp.clip(hi0 - start, 0, count)

        def rows(step, _):
            r0 = jnp.minimum(first + step * 16, count - 16)
            hs = [height_ref[pl.ds(start + r0 + q, 1), :] for q in range(16)]
            for q in range(16):
                film = jnp.concatenate(
                    [
                        ref[1 + row0 + r0 + q].astype(f32),
                        beside(place + r0 + q, second_row),
                    ],
                    axis=1,
                )
                value = (lift_w * hs[q] + lift_b + film).astype(bf16).astype(f32)
                put(0, start + r0 + q, value, d[0])
            return 0

        lax.fori_loop(0, (after - first + 15) // 16, rows, 0)

        @pl.when(jnp.logical_not(valid))
        def _():
            def blank(r, _):
                cat0_ref[start + r] = jnp.zeros((48, WIDE), bf16)
                cat1_ref[start + r] = jnp.zeros((48, WIDE), bf16)
                return 0

            lax.fori_loop(0, count, blank, 0)

    def convs(w, slot, firsts, dil):
        cat = cats[slot]
        rows, sums = [], []
        for r in firsts:
            near = [cat[r - dil], cat[r], cat[r + dil], cat[r + 2 * dil]]
            both = dot(w, jnp.concatenate(near, axis=0))
            rows += [r, r + dil]
            sums += [both[:16], both[16:]]
        return rows, sums

    def parts(pre):
        s = 0.5 + 0.5 * jnp.tanh(0.5 * pre)
        silu = pre * s
        return silu, s + silu * (1.0 - s)

    reach = 2 * total_d
    for l in range(LAYERS - 1):
        slot = l % 2
        w = wf_ref[l]
        bias = wide_row(vec_ref[3 + l])
        reach = reach - d[l]
        lo, hi = bounds(reach)

        def forward(firsts):
            for b, pre in zip(*convs(w, slot, firsts, d[l])):
                silu, slope = parts(pre + bias)
                sp_ref[l, b] = slope
                value = cats[slot][b, 16:32, :].astype(f32) + silu
                put(1 - slot, b, value.astype(bf16).astype(f32), d[l + 1])

        over(lo, hi, d[l], forward)

    sides = (
        [(80 + r, False) for r in range(6)],
        [(86 + r % 3, r >= 3) for r in range(6)],
        [(80 + r, True) for r in range(6)],
    )
    for n, ref in enumerate((u1_ref, own_ref, d1_ref)):
        for half in range(2):
            target, side = jnp.zeros((16, TC), f32), jnp.zeros((16, TC), f32)
            for piece in (half, half + 2, half + 4):
                target = target + ref[33 + piece].astype(f32)
                side = side + beside(*sides[n][piece])
            first = TR * (n + 1) + 16 * half
            height_ref[first : first + 16, :TC] = target
            height_ref[first : first + 16, TC:] = side

    acc_ref[...] = jnp.zeros_like(acc_ref)
    lo, hi = bounds(total_d)
    w3 = wf_ref[3]
    bias3 = wide_row(vec_ref[6])
    readout = wide_row(vec_ref[2])

    def turn(firsts):
        rows, pres = convs(w3, 1, firsts, d[3])
        targets = [height_ref[pl.ds(b, 1), :] for b in rows]
        for b, pre, target in zip(rows, pres, targets):
            silu, slope = parts(pre + bias3)
            value = (cat1_ref[b, 16:32, :].astype(f32) + silu).astype(bf16).astype(f32)
            pressure = jnp.sum(readout * value, axis=0, keepdims=True)
            misfit = pressure - target
            acc_ref[pl.ds(b, 1), :] = misfit * misfit
            adj = readout * (misfit * (1.0 / (SIDE * SIDE)))
            adj_ref[b] = adj
            put(0, b, (adj * slope).astype(bf16).astype(f32), d[3])

    over(lo, hi, d[3], turn)

    reach = total_d
    for l in range(LAYERS - 1, 0, -1):
        slot = (l + 1) % 2
        wb = wb_ref[l]
        reach = reach - d[l]
        lo, hi = bounds(reach)

        def backward(firsts):
            rows, sums = convs(wb, slot, firsts, d[l])
            olds = [adj_ref[b] for b in rows]
            for b, old, change in zip(rows, olds, sums):
                adj = old + change
                adj_ref[b] = adj
                put(1 - slot, b, (adj * sp_ref[l - 1, b]).astype(bf16).astype(f32), d[l - 1])

        over(lo, hi, d[l], backward)

    w0 = wb_ref[0]

    def last(firsts):
        rows, sums = convs(w0, 1, firsts, d[0])
        for b, change in zip(rows, sums):
            adj = adj_ref[b] + change
            hg_ref[pl.ds(b - HALO, 1), :] = jnp.sum(lift_w * adj, axis=0, keepdims=True)

    over(jnp.int32(HALO), jnp.int32(HALO + TR), d[0], last)

    hg = hg_ref[:TR, :TC]
    spans = {-1: (0, 8, 24), 0: (0, 24, 8), 1: (8, 32, 0), 2: (24, 32, 0)}
    message = []
    for block in ((0, 1), (2, -1)):
        lanes = jnp.zeros((1, TC), f32)
        for k in range(2):
            rows = []
            for p in range(NP):
                for dimple in block:
                    lo_r, hi_r, first = spans[dimple]
                    n = hi_r - lo_r
                    prod = hg[lo_r:hi_r] * s2_ref[k, 32 * p + first : 32 * p + first + n, :TC]
                    rows.append(jnp.sum(prod, axis=0, keepdims=True))
            rows += [jnp.zeros((4, TC), f32)]
            sums = jnp.concatenate(rows, axis=0)
            c = iota((TC, TC), 0)
            gather = jnp.where(((c + HALF) // SIDE - k + 1 == spot) & used, 1.0, 0.0)
            z = exact_dot(sums, gather.astype(bf16))
            lanes = lanes + jnp.sum(
                jnp.where(iota((16, TC), 0) == group, z, 0.0), axis=0, keepdims=True
            )
        message.append(lanes)

    def act_ext(dr):
        act = acts[dr, 0]
        act = act + jnp.where(spot == 0, pltpu.roll(acts[dr, -1], 120, 1), 0.0)
        return act + jnp.where(spot == 9, pltpu.roll(acts[dr, 1], 8, 1), 0.0)

    lane = iota((1, TC), 1)
    own_act = act_ext(0)
    ring_act = jnp.where(group % 2 == 0, act_ext(1), act_ext(-1))
    acc = jnp.sum(acc_ref[HALO : HALO + TR, :], axis=0, keepdims=True)
    local = 0.5 * jnp.sum(acc[:, :TC], axis=1, keepdims=True)
    first = jnp.where(used, message[0] * own_act, jnp.where(lane == 120, local, 0.0))
    ring = jnp.where(used, message[1] * ring_act, 0.0)
    whole_message = jnp.concatenate([first, ring], axis=1)
    out_ref[...] = jnp.broadcast_to(whole_message[None], out_ref.shape)


def final_kernel(grid, place_ref, design_ref, gathered2_ref, moved_ref, new_ref, obj_ref, whole_ref):
    row_count, col_count = grid
    whole, squares, misfit2 = combine(gathered2_ref[...].reshape(row_count * col_count, 2 * TC))
    lane = iota((1, 128), 1)
    whole_ref[...] = whole
    entries = float(row_count * col_count * NP * 16)
    cells = float(row_count * col_count * TR * TC)
    dev = place_ref[0] * col_count + place_ref[1]
    moved = moved_ref[...] + rate_of(squares, entries) * whole_ref[pl.ds(dev, 1), :]
    group, _, _ = lane_fields(128)
    by_group = jnp.where(iota((16, 128), 0) == group, moved, 0.0)
    lanes = iota((128, HALF), 0)
    pick = jnp.where((lanes % 10 == iota((128, HALF), 1) + 1) & (lanes < 120), 1.0, 0.0)
    change = exact_dot(by_group, pick.astype(bf16))
    for p in range(NP):
        new_ref[p] = design_ref[p] - change[2 * p : 2 * p + 2]
    misfit1 = jnp.sum(jnp.where(lane == 120, moved_ref[...], 0.0), axis=1, keepdims=True)
    obj_ref[0] = jnp.sum(misfit1) / cells
    obj_ref[1] = jnp.sum(misfit2) / cells


def vmem():
    return pl.BlockSpec(memory_space=pltpu.VMEM)


def smem():
    return pl.BlockSpec(memory_space=pltpu.SMEM)


def shape(dims, kind):
    return jax.ShapeDtypeStruct(dims, kind)


def params(mib):
    return pltpu.CompilerParams(vmem_limit_bytes=mib * MIB)


def on_device(
    row_count, col_count, design, active, stamp_basis, film_field, lift_weight, lift_bias,
    conv_weight, conv_bias, readout, target, dilation,
):
    grid = (row_count, col_count)
    here = jnp.stack([lax.axis_index("rows"), lax.axis_index("cols")]).astype(jnp.int32)
    place = jnp.concatenate([here, dilation])
    one, two, three = pl.pallas_call(
        pack_kernel,
        out_shape=(shape((39, 16, TC), bf16), shape((33, 16, TC), bf16), shape((1, 16, TC), bf16)),
        in_specs=[pl.BlockSpec(memory_space=pltpu.HBM)] * 4,
        out_specs=(vmem(),) * 3,
        scratch_shapes=[
            pltpu.VMEM(film_field.shape, bf16),
            pltpu.VMEM(design.shape, f32),
            pltpu.VMEM(active.shape, jnp.int32),
            pltpu.VMEM(target.shape, f32),
            pltpu.SemaphoreType.DMA((4,)),
        ],
        compiler_params=params(8),
        name="pack",
    )(*[pltpu.with_memory_space_constraint(x, pltpu.HBM) for x in (film_field, design, active, target)])

    def shifted(x, axis, by):
        count = lax.axis_size(axis)
        return lax.ppermute(x, axis, [(i, (i + by) % count) for i in range(count)])

    u1, d1 = shifted(one, "rows", 1), shifted(one, "rows", -1)
    u2, d2 = shifted(two, "rows", 2), shifted(two, "rows", -2)

    s2, expand = pl.pallas_call(
        prep_kernel,
        out_shape=(shape((2, NP * 32, WIDE), f32), shape((2, 384, WIDE), bf16)),
        in_specs=[vmem()],
        out_specs=(vmem(), vmem()),
        compiler_params=params(8),
        name="prep",
    )(stamp_basis.reshape(NP * 32, 32))
    def far(x):
        return jnp.concatenate([shifted(x, "rows", 3), shifted(x, "rows", -3)], axis=0)

    def near(x):
        return jnp.zeros((2, 16, TC), bf16)

    later, d1 = lax.optimization_barrier((dilation, d1))
    amps3 = lax.cond(2 * jnp.sum(later) > HALO - HALF, far, near, three)

    def paired(w):
        return jnp.concatenate(
            [jnp.pad(w, ((0, 0), (0, 0), (0, 48))), jnp.pad(w, ((0, 0), (0, 0), (48, 0)))], axis=1
        )

    wf = jnp.transpose(conv_weight, (0, 2, 1, 3)).reshape(LAYERS, 16, 144)
    wb = jnp.transpose(conv_weight[:, ::-1], (0, 3, 1, 2)).reshape(LAYERS, 16, 144)
    vec = jnp.concatenate(
        [lift_weight[None], lift_bias[None], readout[None], conv_bias], axis=0
    )[:, :, None]
    u1, d1, u2, d2, amps3, place, s2, expand = lax.optimization_barrier(
        (u1, d1, u2, d2, amps3, place, s2, expand)
    )
    tiles = (one, u1, u2, d1, d2, amps3)
    to_right, to_left = pl.pallas_call(
        halve_kernel,
        out_shape=(shape((SIDES, 16, TC), bf16),) * 2,
        in_specs=[vmem()] * 6,
        out_specs=(vmem(),) * 2,
        compiler_params=params(8),
        name="halve",
    )(*tiles)
    from_left = shifted(to_right, "cols", 1)
    from_right = shifted(to_left, "cols", -1)
    scratch = [
        pltpu.VMEM((SPARE + 1, 48, WIDE), bf16),
        pltpu.VMEM((SPARE + 1, 48, WIDE), bf16),
        pltpu.VMEM((LAYERS - 1, ROWS, 16, WIDE), f32),
        pltpu.VMEM((ROWS, 16, WIDE), f32),
        pltpu.VMEM((ROWS, WIDE), f32),
        pltpu.VMEM((TR + HALF, WIDE), f32),
        pltpu.VMEM((2, 112, WIDE), f32),
        pltpu.VMEM((ROWS, WIDE), f32),
    ]
    common = (place, vec, paired(wf), paired(wb), s2, expand, *tiles, from_left, from_right)
    specs = [smem()] + [vmem()] * 13

    def gather(message):
        return lax.all_to_all(message, ("rows", "cols"), 0, 0)

    devices = row_count * col_count
    message_shape = shape((devices, 1, 2 * TC), f32)

    message1 = pl.pallas_call(
        functools.partial(step_kernel, False, grid),
        out_shape=message_shape,
        in_specs=specs,
        out_specs=vmem(),
        scratch_shapes=scratch,
        compiler_params=params(30),
        name="step_one",
    )(*common)
    gathered1 = gather(message1)
    message2, moved = pl.pallas_call(
        functools.partial(step_kernel, True, grid),
        out_shape=(message_shape, shape((1, TC), f32)),
        in_specs=specs + [vmem()],
        out_specs=(vmem(), vmem()),
        scratch_shapes=[pltpu.VMEM((devices, TC), f32)] + scratch,
        compiler_params=params(30),
        name="step_two",
    )(*common, gathered1)
    gathered2 = gather(message2)
    new_design, objective = pl.pallas_call(
        functools.partial(final_kernel, grid),
        out_shape=(shape((NP, 2, HALF), f32), shape((2,), f32)),
        in_specs=[smem()] + [vmem()] * 3,
        out_specs=(vmem(), smem()),
        scratch_shapes=[pltpu.VMEM((devices, TC), f32)],
        compiler_params=params(8),
        name="finish",
    )(place, design, gathered2, moved)
    return new_design, objective


def solution(mesh):
    placed = (
        P(None, "rows", "cols"),
        P("rows", "cols"),
        P(),
        P(None, "rows", "cols"),
        P(),
        P(),
        P(),
        P(),
        P(),
        P("rows", "cols"),
        P(),
    )
    return jax.shard_map(
        functools.partial(on_device, mesh.shape["rows"], mesh.shape["cols"]),
        mesh=mesh,
        in_specs=placed,
        out_specs=(P(None, "rows", "cols"), P()),
        check_vma=False,
    )
```
